32 devices in a mesh: section: 4 (over y, core), expert: 8 (over z, x).
Axes of the slice: x: 2, y: 2, z: 4, core: 2. Of those that a mesh axis runs over, the one named last changes fastest.
Arguments:
- tokens: bfloat16 [1024, 3584], P('expert', 'section'), may hold values from -6 to 6
- expert_ids: int32 [1024, 2], P('expert'), may hold values from 0 to 7, all different within a row; in each aligned block of 128 rows (0 to 127, 128 to 255, ...) at most 48 rows name the same one
- gates: float32 [1024, 2], P('expert'), may hold values from 0.02 to 0.4
- cotangent: bfloat16 [1024, 3584], P('expert', 'section'), may hold values from -6 to 6
- w_gate: bfloat16 [8, 3584, 1024], P('expert', 'section'), may hold values from -0.09375 to 0.09375
- w_up: bfloat16 [8, 3584, 1024], P('expert', 'section'), may hold values from -0.09375 to 0.09375
- w_down: bfloat16 [8, 1024, 3584], P('expert', None, 'section'), may hold values from -0.1875 to 0.1875
Outputs:
- mixed: bfloat16 [1024, 3584], P('expert', 'section')
- token_grads: bfloat16 [1024, 3584], P('expert', 'section')
- down_grads: bfloat16 [8, 1024, 3584], P('expert', None, 'section')
The draws below stay inside these ranges and needn't reach their ends.
Inputs may be any that keep to these rules, and one draw needn't show every extreme that they name: `expert_ids`: within each aligned block of 128 rows no expert is named more than 48 times, a bound that some block reaches; the 2 experts of a row differ.
All inputs are finite; a program needn't handle non-finite values.
Results may differ from the reference program's by a relative error of at most 0.024.
Values may be sent and summed in bfloat16 or wider, within the bound.
A program may use at most 64 MiB of HBM per device.

```python
import math
import jax
import jax.numpy as jnp
import numpy as np
from jax import lax

D = 3584
HID = 1024
TOPK = 2
TOK_DEV = 128
EXPERTS = 8
CAP = 48
DC = 896
TOKENS = 1024
N_SECTION = 4
N_EXPERT = 8


def block_scale(own_key, shape, cuts, smallest, top_value):
    gain, own = 1.0, jax.random.fold_in(own_key, 6)
    for position, blocks in cuts:
        draws = jnp.exp(jax.random.uniform(jax.random.fold_in(own, position), (blocks,), jnp.float32, smallest / len(cuts), top_value / len(cuts)))
        gain = gain * jnp.repeat(draws, shape[position] // blocks).reshape([-1 if axis == position else 1 for axis in range(len(shape))])
    return gain


def shared_out(stream_key, own, number, rows, number_of, top, limit, skew):
    sequence = jax.random.permutation(stream_key, number_of)
    crowded, usual = load_shares(number_of, rows * top, limit, skew, True), load_shares(number_of, rows * top, limit, skew, False)
    places = jnp.arange(number_of)

    def named(sizes, offset_by):
        used = int((sizes > 0).sum())
        fixed = max(1, used // 4)
        shifted = fixed + (places - fixed + offset_by * (used - fixed)) % max(1, number_of - fixed)
        return jnp.zeros((number_of,), jnp.int32).at[sequence[jnp.where(places < fixed, places, shifted)]].set(jnp.asarray(sizes, jnp.int32))

    sizes = jnp.where(number % 4 == 0, named(crowded, number // 4), named(usual, number - number // 4 - 1))
    mixed = jax.random.permutation(jax.random.fold_in(own, 3), number_of)
    giver, sink = mixed[0:number_of // 2 * 2:2], mixed[1:number_of // 2 * 2:2]
    margin = jnp.minimum(sizes[giver] - 1, limit - sizes[sink]) // 2
    margin = jnp.where((giver == sequence[0]) | (sink == sequence[0]) | (sizes[sink] == 0), 0, jnp.maximum(margin, 0))
    shifted = jax.random.randint(jax.random.fold_in(own, 4), (number_of // 2,), 0, 1 << 20) % (margin + 1)
    sizes = sizes.at[giver].add(-shifted).at[sink].add(shifted)
    items = jnp.searchsorted(jnp.cumsum(sizes), jnp.arange(rows * top), side="right").astype(jnp.int32)
    listing = items.reshape(top, rows).T
    listing = listing[jax.random.permutation(jax.random.fold_in(own, 1), rows)]
    offset_by = jax.random.randint(jax.random.fold_in(own, 2), (rows, 1), 0, top)
    return jnp.take_along_axis(listing, (jnp.arange(top)[None, :] + offset_by) % top, axis=1)


def load_shares(number_of, total, reach, slope, full):
    portions = [(1 << 20) // math.isqrt(rank ** slope) + 1 for rank in range(1, number_of + 1)]
    largest = reach if full else min(reach, max(-(-total // number_of), total * portions[0] // sum(portions)))
    least = 1 if total - largest >= number_of - 1 else 0
    holding, spare = [largest] + [least] * (number_of - 1), total - largest - least * (number_of - 1)
    while spare > 0:
        candidates = [i for i in range(1, number_of) if holding[i] < largest] or [i for i in range(1, number_of) if holding[i] < reach]
        mass, remaining = sum([portions[i] for i in candidates]), spare
        for i in candidates:
            more = min(reach - holding[i], max(1, remaining * portions[i] // mass), spare)
            holding[i] = holding[i] + more
            spare = spare - more
    return np.array(holding)


def bell_draw(own_key, dims, width, bound, shards=(), kind=jnp.bfloat16):
    array = width * jax.random.normal(own_key, dims, jnp.float32)
    if shards:
        array = array * block_scale(own_key, dims, shards, -0.22, 0.18)
    return jnp.clip(array, -bound, bound).astype(kind)


def setup_inputs(seed: int = 0) -> dict:
    streams_of = jax.random.split(jax.random.key(seed), 8)
    tokens = bell_draw(streams_of[0], (TOKENS, D), 1.0, 6.0, ((0, 8), (1, 4)))
    expert_ids_keys = jax.random.split(jax.random.fold_in(streams_of[1], 1), TOKENS // TOK_DEV)
    expert_ids_turns = jax.random.permutation(jax.random.fold_in(streams_of[1], 3), TOKENS // TOK_DEV)
    expert_ids = jax.vmap(lambda own, number: shared_out(jax.random.fold_in(streams_of[1], 2), own, number, TOK_DEV, EXPERTS, TOPK, CAP, 2))(expert_ids_keys, expert_ids_turns).reshape((TOKENS, TOPK))
    gates = jnp.clip(jnp.exp(math.log(0.4) - 2.9957323 * jax.random.uniform(streams_of[2], (TOKENS, TOPK), jnp.float32) ** block_scale(streams_of[2], (TOKENS, TOPK), ((0, 8),), -0.2, 0.2)), 0.02, 0.4)
    cotangent = bell_draw(streams_of[3], (TOKENS, D), 1.0, 6.0, ((0, 8), (1, 4)))
    w_gate = bell_draw(streams_of[4], (EXPERTS, D, HID), D ** -0.5, 0.09375, ((0, 8), (1, 4)))
    w_up = bell_draw(streams_of[5], (EXPERTS, D, HID), D ** -0.5, 0.09375, ((0, 8), (1, 4)))
    w_down = bell_draw(streams_of[6], (EXPERTS, HID, D), HID ** -0.5, 0.1875, ((0, 8), (2, 4)))
    return {"tokens": tokens, "expert_ids": expert_ids, "gates": gates, "cotangent": cotangent, "w_gate": w_gate, "w_up": w_up, "w_down": w_down}


def rounded_groups(left, right, form):
    parts = jnp.einsum(form, left, right).astype(jnp.bfloat16)
    return jnp.sum(parts.astype(jnp.float32), axis=0)


def expert_pass(packed):
    rows, grads, gate_w, up_w, down_w = packed
    row_split = rows.astype(jnp.float32).reshape(-1, N_SECTION, DC)
    grad_split = grads.astype(jnp.float32).reshape(-1, N_SECTION, DC)
    gate_pre = rounded_groups(row_split, gate_w.astype(jnp.float32).reshape(N_SECTION, DC, HID), "rsc,sch->srh")
    up_pre = rounded_groups(row_split, up_w.astype(jnp.float32).reshape(N_SECTION, DC, HID), "rsc,sch->srh")
    sigmoid_val = jax.nn.sigmoid(gate_pre)
    activated = gate_pre * sigmoid_val
    hidden = (activated * up_pre).astype(jnp.bfloat16)
    outputs = jnp.dot(hidden, down_w, preferred_element_type=jnp.float32).astype(jnp.bfloat16)
    hidden_grad = rounded_groups(grad_split, down_w.astype(jnp.float32).reshape(HID, N_SECTION, DC), "rsc,hsc->srh")
    down_grad = jnp.dot(hidden.T, grads, preferred_element_type=jnp.float32).astype(jnp.bfloat16)
    gate_grad = (hidden_grad * up_pre * sigmoid_val * (1.0 + gate_pre * (1.0 - sigmoid_val))).astype(jnp.bfloat16)
    up_grad = (hidden_grad * activated).astype(jnp.bfloat16)
    slot_grad = jnp.dot(gate_grad, gate_w.T, preferred_element_type=jnp.float32)
    slot_grad = slot_grad + jnp.dot(up_grad, up_w.T, preferred_element_type=jnp.float32)
    return outputs, slot_grad.astype(jnp.bfloat16), down_grad


def reference(tokens, expert_ids, gates, cotangent, w_gate, w_up, w_down):
    one_hot = (expert_ids[:, :, None] == jnp.arange(EXPERTS, dtype=jnp.int32)[None, None, :]).astype(jnp.int32)
    per_device = one_hot.reshape(N_EXPERT, TOK_DEV * TOPK, EXPERTS)
    earlier = jnp.cumsum(per_device, axis=1) - per_device
    ranks = jnp.sum(earlier * per_device, axis=2).reshape(TOKENS, TOPK)
    source = (jnp.arange(TOKENS, dtype=jnp.int32) // TOK_DEV)[:, None]
    slot_ids = (expert_ids * (EXPERTS * CAP) + source * CAP + ranks).reshape(-1).astype(jnp.int32)
    total_slots = EXPERTS * EXPERTS * CAP
    spread_rows = jnp.repeat(tokens, TOPK, axis=0)
    sent_rows = jnp.zeros((total_slots, D), jnp.bfloat16).at[slot_ids].set(spread_rows)
    scaled = (gates[:, :, None] * cotangent.astype(jnp.float32)[:, None, :]).astype(jnp.bfloat16)
    sent_grads = jnp.zeros((total_slots, D), jnp.bfloat16).at[slot_ids].set(scaled.reshape(TOKENS * TOPK, D))
    outputs, input_grads, down_grads = lax.map(
        expert_pass,
        (sent_rows.reshape(EXPERTS, EXPERTS * CAP, D), sent_grads.reshape(EXPERTS, EXPERTS * CAP, D), w_gate, w_up, w_down))
    picked_out = outputs.reshape(total_slots, D)[slot_ids].astype(jnp.float32).reshape(TOKENS, TOPK, D)
    picked_grad = input_grads.reshape(total_slots, D)[slot_ids].astype(jnp.float32).reshape(TOKENS, TOPK, D)
    mixed = jnp.sum(gates[:, :, None] * picked_out, axis=1).astype(jnp.bfloat16)
    token_grads = jnp.sum(picked_grad, axis=1).astype(jnp.bfloat16)
    return mixed, token_grads, down_grads
```

```python
import functools

import jax
import jax.numpy as jnp
from jax import lax
from jax.experimental import pallas as pl
from jax.experimental.pallas import tpu as pltpu
from jax.sharding import PartitionSpec as P


def local(tokens, expert_ids, gates, cotangent, w_gate, w_up, w_down):
    tok_rows, top_count = expert_ids.shape
    col_span = tokens.shape[1]
    expert_count = lax.axis_size("expert")
    capacity = capacity_of(tok_rows, top_count, expert_count)
    slot_total = expert_count * capacity
    one_hot = (
        expert_ids[:, :, None] == jnp.arange(expert_count, dtype=jnp.int32)[None, None, :]
    ).astype(jnp.int32)
    one_hot = one_hot.reshape(tok_rows * top_count, expert_count)
    pairs = jnp.arange(tok_rows * top_count, dtype=jnp.int32)
    earlier = jnp.dot(
        (pairs[None, :] < pairs[:, None]).astype(jnp.bfloat16),
        one_hot.astype(jnp.bfloat16),
        preferred_element_type=jnp.float32,
    ).astype(jnp.int32)
    ranks = jnp.sum(earlier * one_hot, axis=1)
    slot_ids = expert_ids.reshape(-1) * capacity + ranks
    picker = (slot_ids[:, None] == jnp.arange(slot_total, dtype=jnp.int32)[None, :]).astype(
        jnp.float32
    )
    picker_rows = picker.reshape(tok_rows, top_count, slot_total)
    chooser = jnp.sum(picker_rows, axis=1)
    weigher = jnp.sum(picker_rows * gates[:, :, None], axis=1)
    sent_rows = jnp.dot(
        chooser.T.astype(jnp.bfloat16), tokens, preferred_element_type=jnp.float32
    ).astype(jnp.bfloat16)
    sent_grads = jnp.dot(
        weigher.T, cotangent.astype(jnp.float32), precision=lax.Precision.HIGHEST
    ).astype(jnp.bfloat16)
    routed_rows, routed_grads = (
        lax.all_to_all(sent_rows, "expert", split_axis=0, concat_axis=0, tiled=True),
        lax.all_to_all(sent_grads, "expert", split_axis=0, concat_axis=0, tiled=True),
    )
    gate_w = w_gate[0]
    up_w = w_up[0]
    down_w = w_down[0]
    grad_term = jnp.einsum("rc,hc->rh", routed_grads, down_w, preferred_element_type=jnp.float32)
    gate_term = jnp.dot(routed_rows, gate_w, preferred_element_type=jnp.float32)
    up_term = jnp.dot(routed_rows, up_w, preferred_element_type=jnp.float32)
    gate_pre, up_pre, hidden_grad = (
        lax.psum_scatter(
            gate_term.astype(jnp.bfloat16), "section", scatter_dimension=1, tiled=True
        ).astype(jnp.float32),
        lax.psum_scatter(
            up_term.astype(jnp.bfloat16), "section", scatter_dimension=1, tiled=True
        ).astype(jnp.float32),
        lax.psum_scatter(
            grad_term.astype(jnp.bfloat16), "section", scatter_dimension=1, tiled=True
        ).astype(jnp.float32),
    )
    sigmoid_val = jax.nn.sigmoid(gate_pre)
    activated = gate_pre * sigmoid_val
    hidden = (activated * up_pre).astype(jnp.bfloat16)
    gate_grad = (
        hidden_grad * up_pre * sigmoid_val * (1.0 + gate_pre * (1.0 - sigmoid_val))
    ).astype(jnp.bfloat16)
    up_grad = (hidden_grad * activated).astype(jnp.bfloat16)
    full_hidden, full_gate_grad, full_up_grad = (
        lax.all_gather(hidden, "section", axis=1, tiled=True),
        lax.all_gather(gate_grad, "section", axis=1, tiled=True),
        lax.all_gather(up_grad, "section", axis=1, tiled=True),
    )
    out_rows = jnp.dot(full_hidden, down_w, preferred_element_type=jnp.float32).astype(jnp.bfloat16)
    down_grad = jnp.einsum(
        "rh,rc->hc", full_hidden, routed_grads, preferred_element_type=jnp.float32
    ).astype(jnp.bfloat16)
    slot_grad = jnp.einsum("rh,ch->rc", full_gate_grad, gate_w, preferred_element_type=jnp.float32)
    slot_grad = (
        slot_grad + jnp.einsum("rh,ch->rc", full_up_grad, up_w, preferred_element_type=jnp.float32)
    ).astype(jnp.bfloat16)
    back_out, back_grad = (
        lax.all_to_all(out_rows, "expert", split_axis=0, concat_axis=0, tiled=True),
        lax.all_to_all(slot_grad, "expert", split_axis=0, concat_axis=0, tiled=True),
    )
    picked_out = jnp.dot(picker.astype(jnp.bfloat16), back_out, preferred_element_type=jnp.float32)
    picked_out = picked_out.reshape(tok_rows, top_count, col_span)
    mixed = jnp.sum(gates[:, :, None] * picked_out, axis=1).astype(jnp.bfloat16)
    token_grads = jnp.dot(
        chooser.astype(jnp.bfloat16), back_grad, preferred_element_type=jnp.float32
    ).astype(jnp.bfloat16)
    return (mixed, token_grads, down_grad[None])


MESH = pl.DeviceIdType.MESH
CHUNKS = 4
NEAR = "NM"
NT = (((1,), (1,)), ((), ()))
TN = (((0,), (0,)), ((), ()))
F32 = jnp.float32
BF = jnp.bfloat16
STEPS = (
    "Nf", "Nb", "If", "Ib", "AfM", "SfA", "AfN", "BfM", "BfN", "AbM",
    "Of", "SbA", "Ob", "CfM", "BbM", "AfA", "BfA", "AbN", "CbM", "AbA",
    "DfM", "SfB", "BbA", "CfA", "SbB", "EfM", "CbA", "CfN", "DfA", "AfB",
    "EfA", "BfB", "DbM", "BbN", "DbA", "EbA", "AbB", "BbB", "CfB", "DfN",
    "UfA", "EbM", "CbB", "DfB", "CbN", "EfB", "UbA", "DbB", "DbN", "EbB",
    "EfN", "G3", "UfB", "G0", "G1", "EbN", "UbB", "P", "G2",
)


def expert_kernel(
    n_exp, cap, ids_r, gate_r, tok, cot, wg_h, wu_h, wd_h,
    mixed_o, tgrad_o, dg_o,
    wg, wu, wd, meta, metas, pick, whi, wlo, gcol, nsend, recv, tbuf, rsend,
    part_f, part_b, r1_f, r1_b, s2_f, s2_b, r2_f, r2_b, act_f, act_b, slope, silu_s,
    hbuf, obuf, bnear, rback, rsum, fback, nsum, dgbuf,
    w_sem, meta_ss, meta_rs, n_ss, d_rs, t_ss, t_rs, rl_ss,
    s1_ss, s1_rs, s2_ss, s2_rs, gy_ss, gy_rs, gm_ss, gm_rs, gr_ss, gr_rs,
    b_ss, bn_rs, rb_rs, u_ss, fb_rs, o_sem,
):
    me_e = lax.axis_index("expert")
    me_s = lax.axis_index("section")
    my_z, my_x = me_e // 2, me_e % 2
    oth_z, oth_x = my_z + 1 - 2 * (my_z % 2), 1 - my_x
    side = my_z // 2
    inner = my_z == 1 + side
    far_z = (2 - side, 3 - 3 * side)
    rank_in = (my_z + side + 1) % 2
    first = 4 * side
    my_y, my_c = me_s // 2, me_s % 2
    oth_y, oth_c = 1 - my_y, 1 - my_c
    mate = my_y * 2 + oth_c
    ypart = oth_y * 2 + my_c
    n_tok, cols = tok.shape
    hid = wg.shape[1]
    quarter = hid // 4
    topk = ids_r.shape[0]
    half = (n_exp // 2) * cap

    my_l = (my_z % 2) * 2 + my_x
    near = ((my_z, oth_x), (oth_z, my_x), (oth_z, oth_x))
    near_l = [(z % 2) * 2 + x for z, x in near]

    def at(z, x):
        return (me_s, z * 2 + x)

    def remote(src, dst, ss, rs, dev):
        return pltpu.make_async_remote_copy(
            src_ref=src, dst_ref=dst, send_sem=ss, recv_sem=rs, device_id=dev,
            device_id_type=MESH,
        )

    loads = [
        pltpu.make_async_copy(a, b, w_sem.at[i])
        for i, (a, b) in enumerate(((wg_h, wg), (wu_h, wu), (wd_h, wd)))
    ]
    for load in loads:
        load.start()

    barrier = pltpu.get_barrier_semaphore()
    friends = [at(z, x) for z, x in near] + [at(z, my_x) for z in far_z]
    friends += [(mate, me_e), (ypart, me_e)]
    for dev in friends:
        pl.semaphore_signal(barrier, inc=1, device_id=dev, device_id_type=MESH)

    e_r = lax.broadcasted_iota(jnp.int32, (n_exp, n_tok), 0).astype(F32)
    t0 = lax.broadcasted_iota(jnp.int32, (n_tok, n_tok), 0)
    t1 = lax.broadcasted_iota(jnp.int32, (n_tok, n_tok), 1)
    before = (t0 < t1).astype(BF)
    s_iota = lax.broadcasted_iota(jnp.int32, (half, n_tok), 0)

    def prepare(i, ids, gates):
        hot = [(ids[k : k + 1, :] == e_r).astype(F32) for k in range(topk)]
        base = jnp.dot(sum(hot).astype(BF), before, preferred_element_type=F32) + e_r * cap
        chosen = jnp.zeros((half, n_tok), F32)
        weight = jnp.zeros((half, n_tok), F32)
        for k in range(topk):
            slot = jnp.sum(hot[k] * base, axis=0, keepdims=True).astype(jnp.int32)
            hit = (slot - first * cap == s_iota).astype(F32)
            chosen = chosen + hit
            weight = weight + hit * gates[k : k + 1, :]
            base = base + hot[k]
        pick[i] = chosen.astype(BF)
        high = weight.astype(BF)
        whi[i] = high
        wlo[i] = (weight - high.astype(F32)).astype(BF)
        gcol[i] = jnp.sum(weight, axis=1, keepdims=True)

    def select(i, t, rows):
        got = jnp.dot(pick[i], rows, preferred_element_type=F32)
        if t:
            got = got * gcol[i]
        return got.astype(BF).reshape(n_exp // 2, cap, cols)

    def collect(i, t, rows):
        rows = rows.reshape(half, cols)
        if t:
            return lax.dot_general(pick[i], rows, TN, preferred_element_type=F32)
        return lax.dot_general(whi[i], rows, TN, preferred_element_type=F32) + lax.dot_general(
            wlo[i], rows, TN, preferred_element_type=F32
        )

    def send_meta():
        return remote(
            meta, metas.at[rank_in], meta_ss, meta_rs.at[rank_in], at(far_z[0], my_x)
        )

    def send_block(t):
        return remote(
            (tok, cot)[t], tbuf.at[rank_in, t], t_ss.at[t], t_rs.at[rank_in, t],
            at(far_z[0], my_x),
        )

    def send_near(j, t):
        c = 1 if j else 0
        return remote(
            nsend.at[t, near_l[j]], recv.at[c, my_x, t], n_ss.at[j, t], d_rs.at[c, my_x, t],
            at(*near[j]),
        )

    def send_relay(r, j, t):
        return remote(
            rsend.at[r, t, near_l[j]], recv.at[2 + r, my_x, t], rl_ss.at[r, j, t],
            d_rs.at[2 + r, my_x, t], at(*near[j]),
        )

    def arrived(c, x, t):
        return remote(
            nsend.at[t, 0], recv.at[c, x, t], n_ss.at[0, t], d_rs.at[c, x, t], at(*near[0])
        )

    def give(c, j, t):
        x = oth_x if j else my_x
        src, ss = obuf.at[c, x, t], b_ss.at[c, j, t]
        if c < 2:
            return remote(
                src, bnear.at[t, my_l], ss, bn_rs.at[my_l, t], at(oth_z if c else my_z, x)
            )
        return remote(
            src, rback.at[c - 2, t, my_l], ss, rb_rs.at[c - 2, my_l, t], at(1 + side, x)
        )

    def send_sum(r, t):
        return remote(
            rsum.at[r, t], fback.at[t], u_ss.at[r, t], fb_rs.at[t], at(far_z[r], my_x)
        )

    def to_section(src, dst, ss, rs, s):
        return remote(src, dst, ss, rs, (s, me_e))

    part, r1, s2, r2 = (part_f, part_b), (r1_f, r1_b), (s2_f, s2_b), (r2_f, r2_b)
    act = (act_f, act_b)

    def pair(c):
        return pl.ds(2 * c, 2)

    def rs1(c, t):
        k = 2 * c + t
        return to_section(
            part[t].at[pair(c), oth_c], r1[t].at[pair(c)], s1_ss.at[k], s1_rs.at[k], mate
        )

    def rs2(c, t):
        k = 2 * c + t
        return to_section(s2[t].at[pair(c)], r2[t].at[pair(c)], s2_ss.at[k], s2_rs.at[k], ypart)

    def ag_y(c, t, y=None):
        k = 2 * c + t
        mine = act[t].at[pair(c), my_c, my_y if y is None else y]
        return to_section(mine, mine, gy_ss.at[k], gy_rs.at[k], ypart)

    def ag_m(c, t, core=None):
        k = 2 * c + t
        mine = act[t].at[pair(c), my_c if core is None else core, my_y]
        return to_section(mine, mine, gm_ss.at[k], gm_rs.at[k], mate)

    def ag_r(c, t, core=None):
        k = 2 * c + t
        mine = act[t].at[pair(c), my_c if core is None else core, oth_y]
        return to_section(mine, mine, gr_ss.at[k], gr_rs.at[k], mate)

    def near_step(t):
        picked = select(0, t, (tok, cot)[t][...])
        nsend[t] = picked
        recv[0, my_x, t] = nsend[t, my_l]

    def stage_s(r, t):
        @pl.when(inner)
        def _():
            if not t:
                remote(
                    meta, metas.at[r], meta_ss, meta_rs.at[r], at(far_z[0], my_x)
                ).wait_recv()
                prepare(1 + r, metas[r, 0:topk, :], metas[r, topk : 2 * topk, :])
            remote(
                tok, tbuf.at[r, t], t_ss.at[t], t_rs.at[r, t], at(far_z[0], my_x)
            ).wait_recv()
            rsend[r, t] = select(1 + r, t, tbuf[r, t])
            for j in (2, 1, 0):
                send_relay(r, j, t).start()
            recv[2 + r, my_x, t] = rsend[r, t, my_l]

    def stage_a(c, t):
        arrived(c, oth_x, t).wait_recv()
        if c == 1:
            arrived(c, my_x, t).wait_recv()
        elif c > 1:
            @pl.when(jnp.logical_not(inner))
            def _():
                arrived(c, my_x, t).wait_recv()

        x = recv[c, :, t].reshape(2 * cap, cols)
        for q in range(4):
            span = slice(q * quarter, (q + 1) * quarter)
            if t:
                terms = [lax.dot_general(x, wd[span, :], NT, preferred_element_type=F32)]
            else:
                terms = [jnp.dot(x, w[:, span], preferred_element_type=F32) for w in (wg, wu)]
            for j, term in enumerate(terms):
                part[t][pair(c), q // 2, q % 2, j] = term.astype(BF).reshape(2, cap, quarter)
        rs1(c, t).start()

    def stage_b(c, t):
        b = pair(c)
        rs1(c, t).wait_recv()
        s2[t][b] = (part[t][b, my_c, oth_y].astype(F32) + r1[t][b, oth_y].astype(F32)).astype(BF)
        rs2(c, t).start()

    def stage_c(c, t):
        b = pair(c)
        rs2(c, t).wait_recv()

        def total(j):
            return (
                part[t][b, my_c, my_y, j].astype(F32) + r1[t][b, my_y, j].astype(F32)
                + r2[t][b, j].astype(F32)
            )

        if t:
            hg = total(0)
            act_b[b, my_c, my_y, 0] = (hg * slope[b]).astype(BF)
            act_b[b, my_c, my_y, 1] = (hg * silu_s[b]).astype(BF)
        else:
            pre, up = total(0), total(1)
            sig = jax.nn.sigmoid(pre)
            silu = pre * sig
            act_f[b, my_c, my_y, 0] = (silu * up).astype(BF)
            slope[b] = up * sig * (1.0 + pre * (1.0 - sig))
            silu_s[b] = silu
        ag_y(c, t).start()
        ag_m(c, t).start()

    def stage_d(c, t):
        ag_y(c, t, oth_y).wait_recv()
        ag_r(c, t).start()

    def stage_e(c, t):
        ag_m(c, t, oth_c).wait_recv()
        ag_r(c, t, oth_c).wait_recv()
        full = [
            jnp.concatenate(
                [act[t][pair(c), q // 2, q % 2, j].reshape(2 * cap, quarter) for q in range(4)],
                axis=1,
            )
            for j in range(1 + t)
        ]
        if t:
            out = lax.dot_general(full[0], wg[...], NT, preferred_element_type=F32)
            out = out + lax.dot_general(full[1], wu[...], NT, preferred_element_type=F32)
        else:
            hbuf[c] = full[0].reshape(2, cap, hid)
            out = jnp.dot(full[0], wd[...], preferred_element_type=F32)
        obuf[c, :, t] = out.astype(BF).reshape(2, cap, cols)
        give(c, 1, t).start()
        if c == 0:
            bnear[t, my_l] = obuf[c, my_x, t]
        elif c == 1:
            give(c, 0, t).start()
        else:
            @pl.when(inner)
            def _():
                rback[c - 2, t, my_l] = obuf[c, my_x, t]

            @pl.when(jnp.logical_not(inner))
            def _():
                give(c, 0, t).start()

    def stage_u(r, t):
        @pl.when(inner)
        def _():
            for ld in near_l:
                remote(
                    obuf.at[0, 0, t], rback.at[r, t, ld], b_ss.at[0, 1, t], rb_rs.at[r, ld, t],
                    at(*near[0]),
                ).wait_recv()
            rsum[r, t] = collect(1 + r, t, rback[r, t]).astype(BF)
            send_sum(r, t).start()

    def stage_g(q):
        span = slice(q * quarter, (q + 1) * quarter)
        all_g = recv[:, :, 1].reshape(n_exp * cap, cols)
        hq = hbuf[:, :, :, span].reshape(n_exp * cap, quarter)
        dgbuf[span, :] = lax.dot_general(hq, all_g, TN, preferred_element_type=F32).astype(BF)
        store(q).start()

    def store(q):
        span = pl.ds(q * quarter, quarter)
        return pltpu.make_async_copy(dgbuf.at[span], dg_o.at[span], o_sem.at[q])

    def stage_p():
        for t in range(2):
            for ld in near_l:
                remote(
                    obuf.at[0, 0, t], bnear.at[t, ld], b_ss.at[0, 1, t], bn_rs.at[ld, t],
                    at(*near[0]),
                ).wait_recv()
            nsum[t] = collect(0, t, bnear[t])

    meta[...] = jnp.concatenate(
        [ids_r[...].astype(F32), gate_r[...], jnp.zeros((8 - 2 * topk, n_tok), F32)], axis=0
    )
    prepare(0, ids_r[...].astype(F32), gate_r[...])
    near_step(0)
    pl.semaphore_wait(barrier, len(friends))
    send_meta().start()

    def stage_n(t):
        if t:
            near_step(t)
        for j in (2, 1, 0):
            send_near(j, t).start()

    def stage_t(t, role):
        @pl.when(role)
        def _():
            send_block(t).start()

    outer = jnp.logical_not(inner)
    stages = {
        "A": stage_a, "B": stage_b, "C": stage_c, "D": stage_d, "E": stage_e,
    }
    loaded = False
    for step in STEPS:
        if step[0] == "A" and not loaded:
            for load in loads:
                load.wait()
            loaded = True
        if step == "P":
            stage_p()
        elif step[0] == "N":
            stage_n("fb".index(step[1]))
        elif step[0] in "IO":
            stage_t("fb".index(step[1]), inner if step[0] == "I" else outer)
        elif step[0] == "G":
            stage_g(int(step[1]))
        else:
            t, c = "fb".index(step[1]), "NMAB".index(step[2])
            if step[0] == "S":
                stage_s(c - 2, t)
            elif step[0] == "U":
                stage_u(c - 2, t)
            else:
                stages[step[0]](c, t)

    outs = (mixed_o, tgrad_o)
    for t in range(2):
        remote(
            rsum.at[0, t], fback.at[t], u_ss.at[0, t], fb_rs.at[t], at(far_z[0], my_x)
        ).wait_recv()
        outs[t][...] = (nsum[t] + fback[t].astype(F32)).astype(BF)

    send_meta().wait_send()
    for t in range(2):
        send_block(t).wait_send()
        for j in range(3):
            send_near(j, t).wait_send()
        for c in range(CHUNKS):
            for copy in (rs1(c, t), rs2(c, t), ag_y(c, t), ag_m(c, t), ag_r(c, t)):
                copy.wait_send()
            give(c, 1, t).wait_send()
        give(1, 0, t).wait_send()

    @pl.when(inner)
    def _():
        for t in range(2):
            for r in range(2):
                for j in range(3):
                    send_relay(r, j, t).wait_send()
                send_sum(r, t).wait_send()

    @pl.when(jnp.logical_not(inner))
    def _():
        for t in range(2):
            for c in (2, 3):
                give(c, 0, t).wait_send()

    for q in range(4):
        store(q).wait()


def finish_kernel(mixed_r, tgrad_r, dg_h, mixed_o, tgrad_o, dg_o, dg, sem):
    part = dg_h.shape[0] // CHUNKS
    spans = [pl.ds(i * part, part) for i in range(CHUNKS)]
    ins = [pltpu.make_async_copy(dg_h.at[s], dg.at[s], sem.at[0, i]) for i, s in enumerate(spans)]
    outs = [pltpu.make_async_copy(dg.at[s], dg_o.at[s], sem.at[1, i]) for i, s in enumerate(spans)]
    for copy in ins:
        copy.start()
    mixed_o[...] = mixed_r[...]
    tgrad_o[...] = tgrad_r[...]
    for i in range(CHUNKS):
        ins[i].wait()
        outs[i].start()
    for copy in outs:
        copy.wait()


def fused(tokens, expert_ids, gates, cotangent, w_gate, w_up, w_down):
    n_tok, topk = expert_ids.shape
    cols = tokens.shape[1]
    hid = w_gate.shape[2]
    n_exp, n_sec = lax.axis_size("expert"), lax.axis_size("section")
    cap = capacity_of(n_tok, topk, n_exp)
    quarter = hid // n_sec
    group = n_exp // 2
    vm = pl.BlockSpec(memory_space=pltpu.VMEM)
    hbm = pl.BlockSpec(memory_space=pl.ANY)
    dma = pltpu.SemaphoreType.DMA
    ids_r, gate_r = expert_ids.T, gates.T
    shapes = (
        jax.ShapeDtypeStruct((n_tok, cols), BF),
        jax.ShapeDtypeStruct((n_tok, cols), BF),
        jax.ShapeDtypeStruct((hid, cols), BF),
    )

    def per(j, *lead):
        return pltpu.VMEM((n_exp, *lead, j, cap, quarter), BF)

    results = pl.pallas_call(
        functools.partial(expert_kernel, n_exp, cap),
        out_shape=shapes,
        in_specs=[vm] * 4 + [hbm] * 3,
        out_specs=(vm, vm, hbm),
        scratch_shapes=[
            pltpu.VMEM((cols, hid), BF),
            pltpu.VMEM((cols, hid), BF),
            pltpu.VMEM((hid, cols), BF),
            pltpu.VMEM((8, n_tok), F32),
            pltpu.VMEM((2, 8, n_tok), F32),
            pltpu.VMEM((3, group * cap, n_tok), BF),
            pltpu.VMEM((3, group * cap, n_tok), BF),
            pltpu.VMEM((3, group * cap, n_tok), BF),
            pltpu.VMEM((3, group * cap, 1), F32),
            pltpu.VMEM((2, group, cap, cols), BF),
            pltpu.VMEM((CHUNKS, 2, 2, cap, cols), BF),
            pltpu.VMEM((2, 2, n_tok, cols), BF),
            pltpu.VMEM((2, 2, group, cap, cols), BF),
            per(2, 2, 2), per(1, 2, 2), per(2, 2), per(1, 2), per(2), per(1), per(2), per(1),
            per(1, 2, 2), per(2, 2, 2),
            pltpu.VMEM((n_exp, cap, quarter), F32),
            pltpu.VMEM((n_exp, cap, quarter), F32),
            pltpu.VMEM((CHUNKS, 2, cap, hid), BF),
            pltpu.VMEM((CHUNKS, 2, 2, cap, cols), BF),
            pltpu.VMEM((2, group, cap, cols), BF),
            pltpu.VMEM((2, 2, group, cap, cols), BF),
            pltpu.VMEM((2, 2, n_tok, cols), BF),
            pltpu.VMEM((2, n_tok, cols), BF),
            pltpu.VMEM((2, n_tok, cols), F32),
            pltpu.VMEM((hid, cols), BF),
            dma((3,)), dma, dma((2,)), dma((3, 2)), dma((CHUNKS, 2, 2)), dma((2,)),
            dma((2, 2)), dma((2, 3, 2)),
        ]
        + [dma((2 * CHUNKS,)) for _ in range(10)]
        + [
            dma((CHUNKS, 2, 2)), dma((group, 2)), dma((2, group, 2)), dma((2, 2)), dma((2,)),
            dma((4,)),
        ],
        compiler_params=pltpu.CompilerParams(
            collective_id=0, has_side_effects=True, vmem_limit_bytes=60 * 1024 * 1024
        ),
    )(ids_r, gate_r, tokens, cotangent, w_gate[0], w_up[0], w_down[0])
    mixed, tgrad, dg = pl.pallas_call(
        finish_kernel,
        out_shape=shapes,
        in_specs=[vm, vm, hbm],
        out_specs=(vm, vm, hbm),
        scratch_shapes=[pltpu.VMEM((hid, cols), BF), dma((2, CHUNKS))],
    )(*results)
    return mixed, tgrad, dg[None]


def capacity_of(tok_rows, top_count, expert_count):
    return min(tok_rows, max(2, 3 * tok_rows * top_count // (2 * expert_count)))


def layer(tokens, expert_ids, *rest):
    n_exp, n_sec = lax.axis_size("expert"), lax.axis_size("section")
    n_tok, topk = expert_ids.shape
    cap = capacity_of(n_tok, topk, n_exp)
    hid = rest[2].shape[2]
    tiles = (
        n_exp == 2 * CHUNKS and n_sec == 4 and cap % 16 == 0 and n_tok % 128 == 0
        and tokens.shape[1] % 128 == 0 and hid % (n_sec * 128) == 0
    )
    return (fused if tiles else local)(tokens, expert_ids, *rest)


def solution(mesh):
    placed = (
        P("expert", "section"),
        P("expert", None),
        P("expert", None),
        P("expert", "section"),
        P("expert", "section", None),
        P("expert", "section", None),
        P("expert", None, "section"),
    )
    return jax.shard_map(
        layer,
        mesh=mesh,
        in_specs=placed,
        out_specs=(P("expert", "section"), P("expert", "section"), P("expert", None, "section")),
        check_vma=False,
    )
```

```python
import functools

import jax
import jax.numpy as jnp
from jax import lax
from jax.experimental import pallas as pl
from jax.experimental.pallas import tpu as pltpu
from jax.sharding import PartitionSpec as P


def local(tokens, expert_ids, gates, cotangent, w_gate, w_up, w_down):
    tok_rows, top_count = expert_ids.shape
    col_span = tokens.shape[1]
    expert_count = lax.axis_size("expert")
    capacity = capacity_of(tok_rows, top_count, expert_count)
    slot_total = expert_count * capacity
    one_hot = (
        expert_ids[:, :, None] == jnp.arange(expert_count, dtype=jnp.int32)[None, None, :]
    ).astype(jnp.int32)
    one_hot = one_hot.reshape(tok_rows * top_count, expert_count)
    pairs = jnp.arange(tok_rows * top_count, dtype=jnp.int32)
    earlier = jnp.dot(
        (pairs[None, :] < pairs[:, None]).astype(jnp.bfloat16),
        one_hot.astype(jnp.bfloat16),
        preferred_element_type=jnp.float32,
    ).astype(jnp.int32)
    ranks = jnp.sum(earlier * one_hot, axis=1)
    slot_ids = expert_ids.reshape(-1) * capacity + ranks
    picker = (slot_ids[:, None] == jnp.arange(slot_total, dtype=jnp.int32)[None, :]).astype(
        jnp.float32
    )
    picker_rows = picker.reshape(tok_rows, top_count, slot_total)
    chooser = jnp.sum(picker_rows, axis=1)
    weigher = jnp.sum(picker_rows * gates[:, :, None], axis=1)
    sent_rows = jnp.dot(
        chooser.T.astype(jnp.bfloat16), tokens, preferred_element_type=jnp.float32
    ).astype(jnp.bfloat16)
    sent_grads = jnp.dot(
        weigher.T, cotangent.astype(jnp.float32), precision=lax.Precision.HIGHEST
    ).astype(jnp.bfloat16)
    routed_rows, routed_grads = (
        lax.all_to_all(sent_rows, "expert", split_axis=0, concat_axis=0, tiled=True),
        lax.all_to_all(sent_grads, "expert", split_axis=0, concat_axis=0, tiled=True),
    )
    gate_w = w_gate[0]
    up_w = w_up[0]
    down_w = w_down[0]
    grad_term = jnp.einsum("rc,hc->rh", routed_grads, down_w, preferred_element_type=jnp.float32)
    gate_term = jnp.dot(routed_rows, gate_w, preferred_element_type=jnp.float32)
    up_term = jnp.dot(routed_rows, up_w, preferred_element_type=jnp.float32)
    gate_pre, up_pre, hidden_grad = (
        lax.psum_scatter(
            gate_term.astype(jnp.bfloat16), "section", scatter_dimension=1, tiled=True
        ).astype(jnp.float32),
        lax.psum_scatter(
            up_term.astype(jnp.bfloat16), "section", scatter_dimension=1, tiled=True
        ).astype(jnp.float32),
        lax.psum_scatter(
            grad_term.astype(jnp.bfloat16), "section", scatter_dimension=1, tiled=True
        ).astype(jnp.float32),
    )
    sigmoid_val = jax.nn.sigmoid(gate_pre)
    activated = gate_pre * sigmoid_val
    hidden = (activated * up_pre).astype(jnp.bfloat16)
    gate_grad = (
        hidden_grad * up_pre * sigmoid_val * (1.0 + gate_pre * (1.0 - sigmoid_val))
    ).astype(jnp.bfloat16)
    up_grad = (hidden_grad * activated).astype(jnp.bfloat16)
    full_hidden, full_gate_grad, full_up_grad = (
        lax.all_gather(hidden, "section", axis=1, tiled=True),
        lax.all_gather(gate_grad, "section", axis=1, tiled=True),
        lax.all_gather(up_grad, "section", axis=1, tiled=True),
    )
    out_rows = jnp.dot(full_hidden, down_w, preferred_element_type=jnp.float32).astype(jnp.bfloat16)
    down_grad = jnp.einsum(
        "rh,rc->hc", full_hidden, routed_grads, preferred_element_type=jnp.float32
    ).astype(jnp.bfloat16)
    slot_grad = jnp.einsum("rh,ch->rc", full_gate_grad, gate_w, preferred_element_type=jnp.float32)
    slot_grad = (
        slot_grad + jnp.einsum("rh,ch->rc", full_up_grad, up_w, preferred_element_type=jnp.float32)
    ).astype(jnp.bfloat16)
    back_out, back_grad = (
        lax.all_to_all(out_rows, "expert", split_axis=0, concat_axis=0, tiled=True),
        lax.all_to_all(slot_grad, "expert", split_axis=0, concat_axis=0, tiled=True),
    )
    picked_out = jnp.dot(picker.astype(jnp.bfloat16), back_out, preferred_element_type=jnp.float32)
    picked_out = picked_out.reshape(tok_rows, top_count, col_span)
    mixed = jnp.sum(gates[:, :, None] * picked_out, axis=1).astype(jnp.bfloat16)
    token_grads = jnp.dot(
        chooser.astype(jnp.bfloat16), back_grad, preferred_element_type=jnp.float32
    ).astype(jnp.bfloat16)
    return (mixed, token_grads, down_grad[None])


MESH = pl.DeviceIdType.MESH
CHUNKS = 4
NEAR = "NM"
NT = (((1,), (1,)), ((), ()))
TN = (((0,), (0,)), ((), ()))
F32 = jnp.float32
BF = jnp.bfloat16
STEPS = (
    "Nf", "Nb", "If", "Ib", "AfM", "SfA", "AfN", "BfM", "BfN", "AbM",
    "Of", "SbA", "Ob", "CfM", "BbM", "AfA", "BfA", "AbN", "CbM", "AbA",
    "DfM", "SfB", "BbA", "CfA", "SbB", "EfM", "CbA", "CfN", "DfA", "AfB",
    "EfA", "BfB", "DbM", "BbN", "DbA", "EbA", "AbB", "BbB", "CfB", "DfN",
    "UfA", "EbM", "CbB", "DfB", "CbN", "EfB", "UbA", "DbB", "DbN", "EbB",
    "EfN", "G3", "UfB", "G0", "G1", "EbN", "UbB", "P", "G2",
)


def expert_kernel(
    n_exp, cap, ids_h, gate_h, tok_h, cot_h, wg_h, wu_h, wd_h,
    mixed_o, tgrad_o, dg_o,
    ids_r, gate_r, tok, cot, wg, wu, wd, meta, metas, pick, whi, wlo, gcol, nsend, recv, tbuf, rsend,
    part_f, part_b, r1_f, r1_b, s2_f, s2_b, r2_f, r2_b, act_f, act_b, slope, silu_s,
    hbuf, obuf, bnear, rback, rsum, fback, nsum, dgbuf,
    w_sem, meta_ss, meta_rs, n_ss, d_rs, t_ss, t_rs, rl_ss,
    s1_ss, s1_rs, s2_ss, s2_rs, gy_ss, gy_rs, gm_ss, gm_rs, gr_ss, gr_rs,
    b_ss, bn_rs, rb_rs, u_ss, fb_rs, o_sem,
):
    me_e = lax.axis_index("expert")
    me_s = lax.axis_index("section")
    my_z, my_x = me_e // 2, me_e % 2
    oth_z, oth_x = my_z + 1 - 2 * (my_z % 2), 1 - my_x
    side = my_z // 2
    inner = my_z == 1 + side
    far_z = (2 - side, 3 - 3 * side)
    rank_in = (my_z + side + 1) % 2
    first = 4 * side
    my_y, my_c = me_s // 2, me_s % 2
    oth_y, oth_c = 1 - my_y, 1 - my_c
    mate = my_y * 2 + oth_c
    ypart = oth_y * 2 + my_c
    n_tok, cols = tok.shape
    hid = wg.shape[1]
    quarter = hid // 4
    topk = ids_r.shape[0]
    half = (n_exp // 2) * cap

    my_l = (my_z % 2) * 2 + my_x
    near = ((my_z, oth_x), (oth_z, my_x), (oth_z, oth_x))
    near_l = [(z % 2) * 2 + x for z, x in near]

    def at(z, x):
        return (me_s, z * 2 + x)

    def remote(src, dst, ss, rs, dev):
        return pltpu.make_async_remote_copy(
            src_ref=src, dst_ref=dst, send_sem=ss, recv_sem=rs, device_id=dev,
            device_id_type=MESH,
        )

    outer = jnp.logical_not(inner)
    barrier = pltpu.get_barrier_semaphore()
    friends = [at(far_z[0], my_x)] + [at(z, x) for z, x in near[::-1]]
    friends += [(ypart, me_e), (mate, me_e)]

    @pl.when(inner)
    def _():
        pl.semaphore_signal(
            barrier, inc=1, device_id=at(far_z[1], my_x), device_id_type=MESH
        )

    for dev in friends:
        pl.semaphore_signal(barrier, inc=1, device_id=dev, device_id_type=MESH)

    moves = (
        (ids_h, ids_r), (gate_h, gate_r), (tok_h, tok), (cot_h, cot),
        (wg_h, wg), (wu_h, wu), (wd_h, wd),
    )
    loads = [pltpu.make_async_copy(a, b, w_sem.at[i]) for i, (a, b) in enumerate(moves)]
    for load in loads:
        load.start()

    e_r = lax.broadcasted_iota(jnp.int32, (n_exp, n_tok), 0).astype(F32)
    t0 = lax.broadcasted_iota(jnp.int32, (n_tok, n_tok), 0)
    t1 = lax.broadcasted_iota(jnp.int32, (n_tok, n_tok), 1)
    before = (t0 < t1).astype(BF)
    s_iota = lax.broadcasted_iota(jnp.int32, (half, n_tok), 0)

    def prepare(i, ids, gates):
        hot = [(ids[k : k + 1, :] == e_r).astype(F32) for k in range(topk)]
        base = jnp.dot(sum(hot).astype(BF), before, preferred_element_type=F32) + e_r * cap
        chosen = jnp.zeros((half, n_tok), F32)
        weight = jnp.zeros((half, n_tok), F32)
        for k in range(topk):
            slot = jnp.sum(hot[k] * base, axis=0, keepdims=True).astype(jnp.int32)
            hit = (slot - first * cap == s_iota).astype(F32)
            chosen = chosen + hit
            weight = weight + hit * gates[k : k + 1, :]
            base = base + hot[k]
        pick[i] = chosen.astype(BF)
        high = weight.astype(BF)
        whi[i] = high
        wlo[i] = (weight - high.astype(F32)).astype(BF)
        gcol[i] = jnp.sum(weight, axis=1, keepdims=True)

    def select(i, t, rows):
        got = jnp.dot(pick[i], rows, preferred_element_type=F32)
        if t:
            got = got * gcol[i]
        return got.astype(BF).reshape(n_exp // 2, cap, cols)

    def collect(i, t, rows):
        rows = rows.reshape(half, cols)
        if t:
            return lax.dot_general(pick[i], rows, TN, preferred_element_type=F32)
        return lax.dot_general(whi[i], rows, TN, preferred_element_type=F32) + lax.dot_general(
            wlo[i], rows, TN, preferred_element_type=F32
        )

    def send_meta():
        return remote(
            meta, metas.at[rank_in], meta_ss, meta_rs.at[rank_in], at(far_z[0], my_x)
        )

    def send_block(t):
        return remote(
            (tok, cot)[t], tbuf.at[rank_in, t], t_ss.at[t], t_rs.at[rank_in, t],
            at(far_z[0], my_x),
        )

    def send_near(j, t):
        c = 1 if j else 0
        return remote(
            nsend.at[t, near_l[j]], recv.at[c, my_x, t], n_ss.at[j, t], d_rs.at[c, my_x, t],
            at(*near[j]),
        )

    def send_relay(r, j, t):
        return remote(
            rsend.at[r, t, near_l[j]], recv.at[2 + r, my_x, t], rl_ss.at[r, j, t],
            d_rs.at[2 + r, my_x, t], at(*near[j]),
        )

    def arrived(c, x, t):
        return remote(
            nsend.at[t, 0], recv.at[c, x, t], n_ss.at[0, t], d_rs.at[c, x, t], at(*near[0])
        )

    def give(c, j, t):
        x = oth_x if j else my_x
        src, ss = obuf.at[c, x, t], b_ss.at[c, j, t]
        if c < 2:
            return remote(
                src, bnear.at[t, my_l], ss, bn_rs.at[my_l, t], at(oth_z if c else my_z, x)
            )
        return remote(
            src, rback.at[c - 2, t, my_l], ss, rb_rs.at[c - 2, my_l, t], at(1 + side, x)
        )

    def send_sum(r, t):
        return remote(
            rsum.at[r, t], fback.at[t], u_ss.at[r, t], fb_rs.at[t], at(far_z[r], my_x)
        )

    def to_section(src, dst, ss, rs, s):
        return remote(src, dst, ss, rs, (s, me_e))

    part, r1, s2, r2 = (part_f, part_b), (r1_f, r1_b), (s2_f, s2_b), (r2_f, r2_b)
    act = (act_f, act_b)

    def pair(c):
        return pl.ds(2 * c, 2)

    def rs1(c, t):
        k = 2 * c + t
        return to_section(
            part[t].at[pair(c), oth_c], r1[t].at[pair(c)], s1_ss.at[k], s1_rs.at[k], mate
        )

    def rs2(c, t):
        k = 2 * c + t
        return to_section(s2[t].at[pair(c)], r2[t].at[pair(c)], s2_ss.at[k], s2_rs.at[k], ypart)

    def ag_y(c, t, y=None):
        k = 2 * c + t
        mine = act[t].at[pair(c), my_c, my_y if y is None else y]
        return to_section(mine, mine, gy_ss.at[k], gy_rs.at[k], ypart)

    def ag_m(c, t, core=None):
        k = 2 * c + t
        mine = act[t].at[pair(c), my_c if core is None else core, my_y]
        return to_section(mine, mine, gm_ss.at[k], gm_rs.at[k], mate)

    def ag_r(c, t, core=None):
        k = 2 * c + t
        mine = act[t].at[pair(c), my_c if core is None else core, oth_y]
        return to_section(mine, mine, gr_ss.at[k], gr_rs.at[k], mate)

    def near_step(t):
        picked = select(0, t, (tok, cot)[t][...])
        nsend[t] = picked
        recv[0, my_x, t] = nsend[t, my_l]

    def stage_s(r, t):
        @pl.when(inner)
        def _():
            if not t:
                remote(
                    meta, metas.at[r], meta_ss, meta_rs.at[r], at(far_z[0], my_x)
                ).wait_recv()
                prepare(1 + r, metas[r, 0:topk, :], metas[r, topk : 2 * topk, :])
            remote(
                tok, tbuf.at[r, t], t_ss.at[t], t_rs.at[r, t], at(far_z[0], my_x)
            ).wait_recv()
            rsend[r, t] = select(1 + r, t, tbuf[r, t])
            for j in (2, 1, 0):
                send_relay(r, j, t).start()
            recv[2 + r, my_x, t] = rsend[r, t, my_l]

    def stage_a(c, t):
        arrived(c, oth_x, t).wait_recv()
        if c == 1:
            arrived(c, my_x, t).wait_recv()
        elif c > 1:
            @pl.when(outer)
            def _():
                arrived(c, my_x, t).wait_recv()

        x = recv[c, :, t].reshape(2 * cap, cols)
        for q in range(4):
            span = slice(q * quarter, (q + 1) * quarter)
            if t:
                terms = [lax.dot_general(x, wd[span, :], NT, preferred_element_type=F32)]
            else:
                terms = [jnp.dot(x, w[:, span], preferred_element_type=F32) for w in (wg, wu)]
            for j, term in enumerate(terms):
                part[t][pair(c), q // 2, q % 2, j] = term.astype(BF).reshape(2, cap, quarter)
        rs1(c, t).start()

    def stage_b(c, t):
        b = pair(c)
        rs1(c, t).wait_recv()
        s2[t][b] = (part[t][b, my_c, oth_y].astype(F32) + r1[t][b, oth_y].astype(F32)).astype(BF)
        rs2(c, t).start()

    def stage_c(c, t):
        b = pair(c)
        rs2(c, t).wait_recv()

        def total(j):
            return (
                part[t][b, my_c, my_y, j].astype(F32) + r1[t][b, my_y, j].astype(F32)
                + r2[t][b, j].astype(F32)
            )

        if t:
            hg = total(0)
            act_b[b, my_c, my_y, 0] = (hg * slope[b]).astype(BF)
            act_b[b, my_c, my_y, 1] = (hg * silu_s[b]).astype(BF)
        else:
            pre, up = total(0), total(1)
            sig = jax.nn.sigmoid(pre)
            silu = pre * sig
            act_f[b, my_c, my_y, 0] = (silu * up).astype(BF)
            slope[b] = up * sig * (1.0 + pre * (1.0 - sig))
            silu_s[b] = silu
        ag_y(c, t).start()
        ag_m(c, t).start()

    def stage_d(c, t):
        ag_y(c, t, oth_y).wait_recv()
        ag_r(c, t).start()

    def stage_e(c, t):
        ag_m(c, t, oth_c).wait_recv()
        ag_r(c, t, oth_c).wait_recv()
        full = [
            jnp.concatenate(
                [act[t][pair(c), q // 2, q % 2, j].reshape(2 * cap, quarter) for q in range(4)],
                axis=1,
            )
            for j in range(1 + t)
        ]
        if t:
            out = lax.dot_general(full[0], wg[...], NT, preferred_element_type=F32)
            out = out + lax.dot_general(full[1], wu[...], NT, preferred_element_type=F32)
        else:
            hbuf[c] = full[0].reshape(2, cap, hid)
            out = jnp.dot(full[0], wd[...], preferred_element_type=F32)
        obuf[c, :, t] = out.astype(BF).reshape(2, cap, cols)
        give(c, 1, t).start()
        if c == 0:
            bnear[t, my_l] = obuf[c, my_x, t]
        elif c == 1:
            give(c, 0, t).start()
        else:
            @pl.when(inner)
            def _():
                rback[c - 2, t, my_l] = obuf[c, my_x, t]

            @pl.when(outer)
            def _():
                give(c, 0, t).start()

    def stage_u(r, t):
        @pl.when(inner)
        def _():
            for ld in near_l:
                remote(
                    obuf.at[0, 0, t], rback.at[r, t, ld], b_ss.at[0, 1, t], rb_rs.at[r, ld, t],
                    at(*near[0]),
                ).wait_recv()
            rsum[r, t] = collect(1 + r, t, rback[r, t]).astype(BF)
            send_sum(r, t).start()

    def stage_g(q):
        span = slice(q * quarter, (q + 1) * quarter)
        all_g = recv[:, :, 1].reshape(n_exp * cap, cols)
        hq = hbuf[:, :, :, span].reshape(n_exp * cap, quarter)
        dgbuf[span, :] = lax.dot_general(hq, all_g, TN, preferred_element_type=F32).astype(BF)
        store(q).start()

    def store(q):
        span = pl.ds(q * quarter, quarter)
        return pltpu.make_async_copy(dgbuf.at[span], dg_o.at[span], o_sem.at[q])

    def stage_p():
        for t in range(2):
            for ld in near_l:
                remote(
                    obuf.at[0, 0, t], bnear.at[t, ld], b_ss.at[0, 1, t], bn_rs.at[ld, t],
                    at(*near[0]),
                ).wait_recv()
            nsum[t] = collect(0, t, bnear[t])

    for load in loads[:4]:
        load.wait()
    meta[...] = jnp.concatenate(
        [ids_r[...].astype(F32), gate_r[...], jnp.zeros((8 - 2 * topk, n_tok), F32)], axis=0
    )
    prepare(0, ids_r[...].astype(F32), gate_r[...])
    near_step(0)
    @pl.when(inner)
    def _():
        pl.semaphore_wait(barrier, len(friends) + 1)

    @pl.when(outer)
    def _():
        pl.semaphore_wait(barrier, len(friends))

    send_meta().start()

    def stage_n(t):
        if t:
            near_step(t)
        for j in (2, 1, 0):
            send_near(j, t).start()

    def stage_t(t, role):
        @pl.when(role)
        def _():
            send_block(t).start()

    stages = {
        "A": stage_a, "B": stage_b, "C": stage_c, "D": stage_d, "E": stage_e,
    }
    loaded = False
    for step in STEPS:
        if step[0] == "A" and not loaded:
            for load in loads[4:]:
                load.wait()
            loaded = True
        if step == "P":
            stage_p()
        elif step[0] == "N":
            stage_n("fb".index(step[1]))
        elif step[0] in "IO":
            stage_t("fb".index(step[1]), inner if step[0] == "I" else outer)
        elif step[0] == "G":
            stage_g(int(step[1]))
        else:
            t, c = "fb".index(step[1]), "NMAB".index(step[2])
            if step[0] == "S":
                stage_s(c - 2, t)
            elif step[0] == "U":
                stage_u(c - 2, t)
            else:
                stages[step[0]](c, t)

    outs = (mixed_o, tgrad_o)
    for t in range(2):
        remote(
            rsum.at[0, t], fback.at[t], u_ss.at[0, t], fb_rs.at[t], at(far_z[0], my_x)
        ).wait_recv()
        outs[t][...] = (nsum[t] + fback[t].astype(F32)).astype(BF)

    send_meta().wait_send()
    for t in range(2):
        send_block(t).wait_send()
        for j in range(3):
            send_near(j, t).wait_send()
        for c in range(CHUNKS):
            for copy in (rs1(c, t), rs2(c, t), ag_y(c, t), ag_m(c, t), ag_r(c, t)):
                copy.wait_send()
            give(c, 1, t).wait_send()
        give(1, 0, t).wait_send()

    @pl.when(inner)
    def _():
        for t in range(2):
            for r in range(2):
                for j in range(3):
                    send_relay(r, j, t).wait_send()
                send_sum(r, t).wait_send()

    @pl.when(outer)
    def _():
        for t in range(2):
            for c in (2, 3):
                give(c, 0, t).wait_send()

    for q in range(4):
        store(q).wait()


def finish_kernel(mixed_r, tgrad_r, dg_h, mixed_o, tgrad_o, dg_o, sem):
    part = dg_h.shape[0] // CHUNKS
    spans = [pl.ds(i * part, part) for i in range(CHUNKS)]
    outs = [pltpu.make_async_copy(dg_h.at[s], dg_o.at[s], sem.at[i]) for i, s in enumerate(spans)]
    for copy in outs:
        copy.start()
    mixed_o[...] = mixed_r[...]
    tgrad_o[...] = tgrad_r[...]
    for copy in outs:
        copy.wait()


def fused(tokens, expert_ids, gates, cotangent, w_gate, w_up, w_down):
    n_tok, topk = expert_ids.shape
    cols = tokens.shape[1]
    hid = w_gate.shape[2]
    n_exp, n_sec = lax.axis_size("expert"), lax.axis_size("section")
    cap = capacity_of(n_tok, topk, n_exp)
    quarter = hid // n_sec
    group = n_exp // 2
    vm = pl.BlockSpec(memory_space=pltpu.VMEM)
    hbm = pl.BlockSpec(memory_space=pl.ANY)
    dma = pltpu.SemaphoreType.DMA
    ids_r, gate_r = expert_ids.T, gates.T
    shapes = (
        jax.ShapeDtypeStruct((n_tok, cols), BF),
        jax.ShapeDtypeStruct((n_tok, cols), BF),
        jax.ShapeDtypeStruct((hid, cols), BF),
    )

    def per(j, *lead):
        return pltpu.VMEM((n_exp, *lead, j, cap, quarter), BF)

    results = pl.pallas_call(
        functools.partial(expert_kernel, n_exp, cap),
        out_shape=shapes,
        in_specs=[pl.BlockSpec(memory_space=pltpu.HBM)] * 7,
        out_specs=(vm, vm, hbm),
        scratch_shapes=[
            pltpu.VMEM((topk, n_tok), jnp.int32),
            pltpu.VMEM((topk, n_tok), F32),
            pltpu.VMEM((n_tok, cols), BF),
            pltpu.VMEM((n_tok, cols), BF),
            pltpu.VMEM((cols, hid), BF),
            pltpu.VMEM((cols, hid), BF),
            pltpu.VMEM((hid, cols), BF),
            pltpu.VMEM((8, n_tok), F32),
            pltpu.VMEM((2, 8, n_tok), F32),
            pltpu.VMEM((3, group * cap, n_tok), BF),
            pltpu.VMEM((3, group * cap, n_tok), BF),
            pltpu.VMEM((3, group * cap, n_tok), BF),
            pltpu.VMEM((3, group * cap, 1), F32),
            pltpu.VMEM((2, group, cap, cols), BF),
            pltpu.VMEM((CHUNKS, 2, 2, cap, cols), BF),
            pltpu.VMEM((2, 2, n_tok, cols), BF),
            pltpu.VMEM((2, 2, group, cap, cols), BF),
            per(2, 2, 2), per(1, 2, 2), per(2, 2), per(1, 2), per(2), per(1), per(2), per(1),
            per(1, 2, 2), per(2, 2, 2),
            pltpu.VMEM((n_exp, cap, quarter), F32),
            pltpu.VMEM((n_exp, cap, quarter), F32),
            pltpu.VMEM((CHUNKS, 2, cap, hid), BF),
            pltpu.VMEM((CHUNKS, 2, 2, cap, cols), BF),
            pltpu.VMEM((2, group, cap, cols), BF),
            pltpu.VMEM((2, 2, group, cap, cols), BF),
            pltpu.VMEM((2, 2, n_tok, cols), BF),
            pltpu.VMEM((2, n_tok, cols), BF),
            pltpu.VMEM((2, n_tok, cols), F32),
            pltpu.VMEM((hid, cols), BF),
            dma((7,)), dma, dma((2,)), dma((3, 2)), dma((CHUNKS, 2, 2)), dma((2,)),
            dma((2, 2)), dma((2, 3, 2)),
        ]
        + [dma((2 * CHUNKS,)) for _ in range(10)]
        + [
            dma((CHUNKS, 2, 2)), dma((group, 2)), dma((2, group, 2)), dma((2, 2)), dma((2,)),
            dma((4,)),
        ],
        compiler_params=pltpu.CompilerParams(
            collective_id=0, has_side_effects=True, vmem_limit_bytes=40 * 1024 * 1024
        ),
    )(
        *[
            pltpu.with_memory_space_constraint(x, pltpu.HBM)
            for x in (ids_r, gate_r, tokens, cotangent, w_gate[0], w_up[0], w_down[0])
        ]
    )
    mixed, tgrad, dg = pl.pallas_call(
        finish_kernel,
        out_shape=shapes,
        in_specs=[vm, vm, hbm],
        out_specs=(vm, vm, hbm),
        scratch_shapes=[dma((CHUNKS,))],
        compiler_params=pltpu.CompilerParams(vmem_limit_bytes=8 * 1024 * 1024),
    )(*results)
    return mixed, tgrad, dg[None]


def capacity_of(tok_rows, top_count, expert_count):
    return min(tok_rows, max(2, 3 * tok_rows * top_count // (2 * expert_count)))


def layer(tokens, expert_ids, *rest):
    n_exp, n_sec = lax.axis_size("expert"), lax.axis_size("section")
    n_tok, topk = expert_ids.shape
    cap = capacity_of(n_tok, topk, n_exp)
    hid = rest[2].shape[2]
    tiles = (
        n_exp == 2 * CHUNKS and n_sec == 4 and cap % 16 == 0 and n_tok % 128 == 0
        and tokens.shape[1] % 128 == 0 and hid % (n_sec * 128) == 0
    )
    return (fused if tiles else local)(tokens, expert_ids, *rest)


def solution(mesh):
    placed = (
        P("expert", "section"),
        P("expert", None),
        P("expert", None),
        P("expert", "section"),
        P("expert", "section", None),
        P("expert", "section", None),
        P("expert", None, "section"),
    )
    return jax.shard_map(
        layer,
        mesh=mesh,
        in_specs=placed,
        out_specs=(P("expert", "section"), P("expert", "section"), P("expert", None, "section")),
        check_vma=False,
    )
```

```python
import functools

import jax
import jax.numpy as jnp
from jax import lax
from jax.experimental import pallas as pl
from jax.experimental.pallas import tpu as pltpu
from jax.sharding import PartitionSpec as P


def local(tokens, expert_ids, gates, cotangent, w_gate, w_up, w_down):
    tok_rows, top_count = expert_ids.shape
    col_span = tokens.shape[1]
    expert_count = lax.axis_size("expert")
    capacity = capacity_of(tok_rows, top_count, expert_count)
    slot_total = expert_count * capacity
    one_hot = (
        expert_ids[:, :, None] == jnp.arange(expert_count, dtype=jnp.int32)[None, None, :]
    ).astype(jnp.int32)
    one_hot = one_hot.reshape(tok_rows * top_count, expert_count)
    pairs = jnp.arange(tok_rows * top_count, dtype=jnp.int32)
    earlier = jnp.dot(
        (pairs[None, :] < pairs[:, None]).astype(jnp.bfloat16),
        one_hot.astype(jnp.bfloat16),
        preferred_element_type=jnp.float32,
    ).astype(jnp.int32)
    ranks = jnp.sum(earlier * one_hot, axis=1)
    slot_ids = expert_ids.reshape(-1) * capacity + ranks
    picker = (slot_ids[:, None] == jnp.arange(slot_total, dtype=jnp.int32)[None, :]).astype(
        jnp.float32
    )
    picker_rows = picker.reshape(tok_rows, top_count, slot_total)
    chooser = jnp.sum(picker_rows, axis=1)
    weigher = jnp.sum(picker_rows * gates[:, :, None], axis=1)
    sent_rows = jnp.dot(
        chooser.T.astype(jnp.bfloat16), tokens, preferred_element_type=jnp.float32
    ).astype(jnp.bfloat16)
    sent_grads = jnp.dot(
        weigher.T, cotangent.astype(jnp.float32), precision=lax.Precision.HIGHEST
    ).astype(jnp.bfloat16)
    routed_rows, routed_grads = (
        lax.all_to_all(sent_rows, "expert", split_axis=0, concat_axis=0, tiled=True),
        lax.all_to_all(sent_grads, "expert", split_axis=0, concat_axis=0, tiled=True),
    )
    gate_w = w_gate[0]
    up_w = w_up[0]
    down_w = w_down[0]
    grad_term = jnp.einsum("rc,hc->rh", routed_grads, down_w, preferred_element_type=jnp.float32)
    gate_term = jnp.dot(routed_rows, gate_w, preferred_element_type=jnp.float32)
    up_term = jnp.dot(routed_rows, up_w, preferred_element_type=jnp.float32)
    gate_pre, up_pre, hidden_grad = (
        lax.psum_scatter(
            gate_term.astype(jnp.bfloat16), "section", scatter_dimension=1, tiled=True
        ).astype(jnp.float32),
        lax.psum_scatter(
            up_term.astype(jnp.bfloat16), "section", scatter_dimension=1, tiled=True
        ).astype(jnp.float32),
        lax.psum_scatter(
            grad_term.astype(jnp.bfloat16), "section", scatter_dimension=1, tiled=True
        ).astype(jnp.float32),
    )
    sigmoid_val = jax.nn.sigmoid(gate_pre)
    activated = gate_pre * sigmoid_val
    hidden = (activated * up_pre).astype(jnp.bfloat16)
    gate_grad = (
        hidden_grad * up_pre * sigmoid_val * (1.0 + gate_pre * (1.0 - sigmoid_val))
    ).astype(jnp.bfloat16)
    up_grad = (hidden_grad * activated).astype(jnp.bfloat16)
    full_hidden, full_gate_grad, full_up_grad = (
        lax.all_gather(hidden, "section", axis=1, tiled=True),
        lax.all_gather(gate_grad, "section", axis=1, tiled=True),
        lax.all_gather(up_grad, "section", axis=1, tiled=True),
    )
    out_rows = jnp.dot(full_hidden, down_w, preferred_element_type=jnp.float32).astype(jnp.bfloat16)
    down_grad = jnp.einsum(
        "rh,rc->hc", full_hidden, routed_grads, preferred_element_type=jnp.float32
    ).astype(jnp.bfloat16)
    slot_grad = jnp.einsum("rh,ch->rc", full_gate_grad, gate_w, preferred_element_type=jnp.float32)
    slot_grad = (
        slot_grad + jnp.einsum("rh,ch->rc", full_up_grad, up_w, preferred_element_type=jnp.float32)
    ).astype(jnp.bfloat16)
    back_out, back_grad = (
        lax.all_to_all(out_rows, "expert", split_axis=0, concat_axis=0, tiled=True),
        lax.all_to_all(slot_grad, "expert", split_axis=0, concat_axis=0, tiled=True),
    )
    picked_out = jnp.dot(picker.astype(jnp.bfloat16), back_out, preferred_element_type=jnp.float32)
    picked_out = picked_out.reshape(tok_rows, top_count, col_span)
    mixed = jnp.sum(gates[:, :, None] * picked_out, axis=1).astype(jnp.bfloat16)
    token_grads = jnp.dot(
        chooser.astype(jnp.bfloat16), back_grad, preferred_element_type=jnp.float32
    ).astype(jnp.bfloat16)
    return (mixed, token_grads, down_grad[None])


MESH = pl.DeviceIdType.MESH
CHUNKS = 4
NEAR = "NM"
NT = (((1,), (1,)), ((), ()))
TN = (((0,), (0,)), ((), ()))
F32 = jnp.float32
BF = jnp.bfloat16
STEPS = (
    "If", "Nf", "Nb", "Ib", "SfA0", "AfM", "BfM", "AfN", "SfA1", "AbN",
    "Of", "AbM", "BfN", "Ob", "SbA0", "CfM", "BbM", "SbA1", "BbN", "AfA",
    "SfB0", "BfA", "DfM", "CfN", "AbA", "SfB1", "BbA", "SbB0", "CfA", "EfM",
    "CbA", "AfB", "DfA", "BfB", "SbB1", "EfA", "CbM", "DbA", "EbA", "CfB",
    "AbB", "UfA0", "DbM", "BbB", "DfB", "DfN", "UfA1", "CbN", "EfB", "UbA0",
    "EbM", "CbB", "EfN", "G0", "UbA1", "G3", "G2", "DbN", "UfB0", "DbB",
    "EbB", "UfB1", "EbN", "UbB0", "UbB1", "G1", "P",
)


def expert_kernel(
    n_exp, cap, ids_h, gate_h, tok_h, cot_h, wg_h, wu_h, wd_h,
    mixed_o, tgrad_o, dg_o,
    ids_r, gate_r, tok, cot, wg, wu, wd, meta, metas, pick, whi, wlo, gcol, nsend, recv, tbuf, rsend,
    part_f, part_b, r1_f, r1_b, s2_f, s2_b, r2_f, r2_b, act_f, act_b, slope, silu_s,
    hbuf, obuf, bnear, rback, rsum, fback, nsum, dgbuf,
    w_sem, meta_ss, meta_rs, n_ss, d_rs, t_ss, t_rs, rl_ss, dx_rs,
    s1_ss, s1_rs, s2_ss, s2_rs, gy_ss, gy_rs, gm_ss, gm_rs, gr_ss, gr_rs,
    b_ss, bx_ss, bn_rs, rb_rs, u_ss, fb_rs, o_sem,
):
    me_e = lax.axis_index("expert")
    me_s = lax.axis_index("section")
    my_z, my_x = me_e // 2, me_e % 2
    oth_z, oth_x = my_z + 1 - 2 * (my_z % 2), 1 - my_x
    side = my_z // 2
    inner = my_z == 1 + side
    far_z = (2 - side, 3 - 3 * side)
    rank_in = (my_z + side + 1) % 2
    first = 4 * side
    my_y, my_c = me_s // 2, me_s % 2
    oth_y, oth_c = 1 - my_y, 1 - my_c
    mate = my_y * 2 + oth_c
    ypart = oth_y * 2 + my_c
    n_tok, cols = tok.shape
    hid = wg.shape[1]
    quarter = hid // 4
    topk = ids_r.shape[0]
    half = (n_exp // 2) * cap
    cut = (cols // 128 + 1) // 2 * 128
    spans = (slice(0, cut), slice(cut, cols))
    parts = (pl.ds(0, cut), pl.ds(cut, cols - cut))

    my_l = (my_z % 2) * 2 + my_x
    near = ((my_z, oth_x), (oth_z, my_x), (oth_z, oth_x))
    near_l = [(z % 2) * 2 + x for z, x in near]

    def at(z, x):
        return (me_s, z * 2 + x)

    def remote(src, dst, ss, rs, dev):
        return pltpu.make_async_remote_copy(
            src_ref=src, dst_ref=dst, send_sem=ss, recv_sem=rs, device_id=dev,
            device_id_type=MESH,
        )

    outer = jnp.logical_not(inner)
    barrier = pltpu.get_barrier_semaphore()
    friends = [at(far_z[0], my_x)] + [at(z, x) for z, x in near[::-1]]
    friends += [(ypart, me_e), (mate, me_e)]

    @pl.when(inner)
    def _():
        pl.semaphore_signal(
            barrier, inc=1, device_id=at(far_z[1], my_x), device_id_type=MESH
        )

    for dev in friends:
        pl.semaphore_signal(barrier, inc=1, device_id=dev, device_id_type=MESH)

    moves = (
        (ids_h, ids_r), (gate_h, gate_r), (tok_h, tok), (cot_h, cot),
        (wg_h, wg), (wu_h, wu), (wd_h, wd),
    )
    loads = [pltpu.make_async_copy(a, b, w_sem.at[i]) for i, (a, b) in enumerate(moves)]
    for load in loads:
        load.start()

    e_r = lax.broadcasted_iota(jnp.int32, (n_exp, n_tok), 0).astype(F32)
    t0 = lax.broadcasted_iota(jnp.int32, (n_tok, n_tok), 0)
    t1 = lax.broadcasted_iota(jnp.int32, (n_tok, n_tok), 1)
    before = (t0 < t1).astype(BF)
    s_iota = lax.broadcasted_iota(jnp.int32, (half, n_tok), 0)

    def prepare(i, ids, gates):
        hot = [(ids[k : k + 1, :] == e_r).astype(F32) for k in range(topk)]
        base = jnp.dot(sum(hot).astype(BF), before, preferred_element_type=F32) + e_r * cap
        chosen = jnp.zeros((half, n_tok), F32)
        weight = jnp.zeros((half, n_tok), F32)
        for k in range(topk):
            slot = jnp.sum(hot[k] * base, axis=0, keepdims=True).astype(jnp.int32)
            hit = (slot - first * cap == s_iota).astype(F32)
            chosen = chosen + hit
            weight = weight + hit * gates[k : k + 1, :]
            base = base + hot[k]
        pick[i] = chosen.astype(BF)
        high = weight.astype(BF)
        whi[i] = high
        wlo[i] = (weight - high.astype(F32)).astype(BF)
        gcol[i] = jnp.sum(weight, axis=1, keepdims=True)

    def select(i, t, rows):
        got = jnp.dot(pick[i], rows, preferred_element_type=F32)
        if t:
            got = got * gcol[i]
        return got.astype(BF).reshape(n_exp // 2, cap, rows.shape[-1])

    def collect(i, t, rows):
        rows = rows.reshape(half, rows.shape[-1])
        if t:
            return lax.dot_general(pick[i], rows, TN, preferred_element_type=F32)
        return lax.dot_general(whi[i], rows, TN, preferred_element_type=F32) + lax.dot_general(
            wlo[i], rows, TN, preferred_element_type=F32
        )

    def send_meta():
        return remote(
            meta, metas.at[rank_in], meta_ss, meta_rs.at[rank_in], at(far_z[0], my_x)
        )

    def send_block(t, h):
        return remote(
            (tok, cot)[t].at[:, parts[h]], tbuf.at[rank_in, t, :, parts[h]], t_ss.at[t, h],
            t_rs.at[rank_in, t, h], at(far_z[0], my_x),
        )

    def send_near(j, t):
        c = 1 if j else 0
        return remote(
            nsend.at[t, near_l[j]], recv.at[c, my_x, t], n_ss.at[j, t], d_rs.at[c, my_x, t],
            at(*near[j]),
        )

    def send_relay(r, j, t, h):
        return remote(
            rsend.at[r, t, near_l[j], :, parts[h]], recv.at[2 + r, my_x, t, :, parts[h]],
            rl_ss.at[r, j, t, h], dx_rs.at[r, my_x, t, h], at(*near[j]),
        )

    def relayed(r, x, t, h):
        return remote(
            rsend.at[r, t, 0, :, parts[h]], recv.at[2 + r, x, t, :, parts[h]],
            rl_ss.at[r, 0, t, h], dx_rs.at[r, x, t, h], at(*near[0]),
        )

    def arrived(c, x, t):
        return remote(
            nsend.at[t, 0], recv.at[c, x, t], n_ss.at[0, t], d_rs.at[c, x, t], at(*near[0])
        )

    def give(c, j, t):
        x = oth_x if j else my_x
        return remote(
            obuf.at[c, x, t], bnear.at[t, my_l], b_ss.at[c, j, t], bn_rs.at[my_l, t],
            at(oth_z if c else my_z, x),
        )

    def pass_on(r, j, t, h):
        x = oth_x if j else my_x
        return remote(
            obuf.at[2 + r, x, t, :, parts[h]], rback.at[r, t, my_l, :, parts[h]],
            bx_ss.at[r, j, t, h], rb_rs.at[r, my_l, t, h], at(1 + side, x),
        )

    def send_sum(r, t, h):
        return remote(
            rsum.at[r, t, :, parts[h]], fback.at[t, :, parts[h]], u_ss.at[r, t, h],
            fb_rs.at[t, h], at(far_z[r], my_x),
        )

    def to_section(src, dst, ss, rs, s):
        return remote(src, dst, ss, rs, (s, me_e))

    part, r1, s2, r2 = (part_f, part_b), (r1_f, r1_b), (s2_f, s2_b), (r2_f, r2_b)
    act = (act_f, act_b)

    def pair(c):
        return pl.ds(2 * c, 2)

    def rs1(c, t):
        k = 2 * c + t
        return to_section(
            part[t].at[pair(c), oth_c], r1[t].at[pair(c)], s1_ss.at[k], s1_rs.at[k], mate
        )

    def rs2(c, t):
        k = 2 * c + t
        return to_section(s2[t].at[pair(c)], r2[t].at[pair(c)], s2_ss.at[k], s2_rs.at[k], ypart)

    def ag_y(c, t, y=None):
        k = 2 * c + t
        mine = act[t].at[pair(c), my_c, my_y if y is None else y]
        return to_section(mine, mine, gy_ss.at[k], gy_rs.at[k], ypart)

    def ag_m(c, t, core=None):
        k = 2 * c + t
        mine = act[t].at[pair(c), my_c if core is None else core, my_y]
        return to_section(mine, mine, gm_ss.at[k], gm_rs.at[k], mate)

    def ag_r(c, t, core=None):
        k = 2 * c + t
        mine = act[t].at[pair(c), my_c if core is None else core, oth_y]
        return to_section(mine, mine, gr_ss.at[k], gr_rs.at[k], mate)

    def near_step(t):
        picked = select(0, t, (tok, cot)[t][...])
        nsend[t] = picked
        recv[0, my_x, t] = nsend[t, my_l]

    def stage_s(r, t, h):
        @pl.when(inner)
        def _():
            if not t and not h:
                remote(
                    meta, metas.at[r], meta_ss, meta_rs.at[r], at(far_z[0], my_x)
                ).wait_recv()
                prepare(1 + r, metas[r, 0:topk, :], metas[r, topk : 2 * topk, :])
            remote(
                tok.at[:, parts[h]], tbuf.at[r, t, :, parts[h]], t_ss.at[t, h],
                t_rs.at[r, t, h], at(far_z[0], my_x),
            ).wait_recv()
            rsend[r, t, :, :, spans[h]] = select(1 + r, t, tbuf[r, t, :, spans[h]])
            for j in (2, 1, 0):
                send_relay(r, j, t, h).start()
            recv[2 + r, my_x, t, :, spans[h]] = rsend[r, t, my_l, :, spans[h]]

    def stage_a(c, t):
        if c < 2:
            arrived(c, oth_x, t).wait_recv()
            if c == 1:
                arrived(c, my_x, t).wait_recv()
        else:
            for h in range(2):
                relayed(c - 2, oth_x, t, h).wait_recv()

            @pl.when(outer)
            def _():
                for h in range(2):
                    relayed(c - 2, my_x, t, h).wait_recv()

        x = recv[c, :, t].reshape(2 * cap, cols)
        for q in range(4):
            span = slice(q * quarter, (q + 1) * quarter)
            if t:
                terms = [lax.dot_general(x, wd[span, :], NT, preferred_element_type=F32)]
            else:
                terms = [jnp.dot(x, w[:, span], preferred_element_type=F32) for w in (wg, wu)]
            for j, term in enumerate(terms):
                part[t][pair(c), q // 2, q % 2, j] = term.astype(BF).reshape(2, cap, quarter)
        rs1(c, t).start()

    def stage_b(c, t):
        b = pair(c)
        rs1(c, t).wait_recv()
        s2[t][b] = (part[t][b, my_c, oth_y].astype(F32) + r1[t][b, oth_y].astype(F32)).astype(BF)
        rs2(c, t).start()

    def stage_c(c, t):
        b = pair(c)
        rs2(c, t).wait_recv()

        def total(j):
            return (
                part[t][b, my_c, my_y, j].astype(F32) + r1[t][b, my_y, j].astype(F32)
                + r2[t][b, j].astype(F32)
            )

        if t:
            hg = total(0)
            act_b[b, my_c, my_y, 0] = (hg * slope[b]).astype(BF)
            act_b[b, my_c, my_y, 1] = (hg * silu_s[b]).astype(BF)
        else:
            pre, up = total(0), total(1)
            sig = jax.nn.sigmoid(pre)
            silu = pre * sig
            act_f[b, my_c, my_y, 0] = (silu * up).astype(BF)
            slope[b] = up * sig * (1.0 + pre * (1.0 - sig))
            silu_s[b] = silu
        ag_y(c, t).start()
        ag_m(c, t).start()

    def stage_d(c, t):
        ag_y(c, t, oth_y).wait_recv()
        ag_r(c, t).start()

    def stage_e(c, t):
        ag_m(c, t, oth_c).wait_recv()
        ag_r(c, t, oth_c).wait_recv()
        full = [
            jnp.concatenate(
                [act[t][pair(c), q // 2, q % 2, j].reshape(2 * cap, quarter) for q in range(4)],
                axis=1,
            )
            for j in range(1 + t)
        ]
        if not t:
            hbuf[c] = full[0].reshape(2, cap, hid)

        def product(span):
            if t:
                out = lax.dot_general(full[0], wg[span, :], NT, preferred_element_type=F32)
                out = out + lax.dot_general(
                    full[1], wu[span, :], NT, preferred_element_type=F32
                )
            else:
                out = jnp.dot(full[0], wd[:, span], preferred_element_type=F32)
            return out.astype(BF).reshape(2, cap, out.shape[-1])

        if c < 2:
            obuf[c, :, t] = product(slice(0, cols))
            give(c, 1, t).start()
            if c:
                give(c, 0, t).start()
            else:
                bnear[t, my_l] = obuf[c, my_x, t]
            return
        for h in range(2):
            obuf[c, :, t, :, spans[h]] = product(spans[h])
            pass_on(c - 2, 1, t, h).start()

            @pl.when(inner)
            def _(h=h):
                rback[c - 2, t, my_l, :, spans[h]] = obuf[c, my_x, t, :, spans[h]]

            @pl.when(outer)
            def _(h=h):
                pass_on(c - 2, 0, t, h).start()

    def stage_u(r, t, h):
        @pl.when(inner)
        def _():
            for ld in near_l:
                remote(
                    obuf.at[2, 0, t, :, parts[h]], rback.at[r, t, ld, :, parts[h]],
                    bx_ss.at[0, 1, t, h], rb_rs.at[r, ld, t, h], at(*near[0]),
                ).wait_recv()
            rsum[r, t, :, spans[h]] = collect(1 + r, t, rback[r, t, :, :, spans[h]]).astype(BF)
            send_sum(r, t, h).start()

    def stage_g(q):
        span = slice(q * quarter, (q + 1) * quarter)
        all_g = recv[:, :, 1].reshape(n_exp * cap, cols)
        hq = hbuf[:, :, :, span].reshape(n_exp * cap, quarter)
        dgbuf[span, :] = lax.dot_general(hq, all_g, TN, preferred_element_type=F32).astype(BF)
        store(q).start()

    def store(q):
        span = pl.ds(q * quarter, quarter)
        return pltpu.make_async_copy(dgbuf.at[span], dg_o.at[span], o_sem.at[q])

    def stage_p():
        for t in range(2):
            for ld in near_l:
                remote(
                    obuf.at[0, 0, t], bnear.at[t, ld], b_ss.at[0, 1, t], bn_rs.at[ld, t],
                    at(*near[0]),
                ).wait_recv()
            nsum[t] = collect(0, t, bnear[t])

    for load in loads[:4]:
        load.wait()
    meta[...] = jnp.concatenate(
        [ids_r[...].astype(F32), gate_r[...], jnp.zeros((8 - 2 * topk, n_tok), F32)], axis=0
    )
    prepare(0, ids_r[...].astype(F32), gate_r[...])
    near_step(0)
    @pl.when(inner)
    def _():
        pl.semaphore_wait(barrier, len(friends) + 1)

    @pl.when(outer)
    def _():
        pl.semaphore_wait(barrier, len(friends))

    send_meta().start()

    def stage_n(t):
        if t:
            near_step(t)
        for j in (2, 1, 0):
            send_near(j, t).start()

    def stage_t(t, role):
        @pl.when(role)
        def _():
            for h in range(2):
                send_block(t, h).start()

    stages = {
        "A": stage_a, "B": stage_b, "C": stage_c, "D": stage_d, "E": stage_e,
    }
    loaded = False
    for step in STEPS:
        if step[0] == "A" and not loaded:
            for load in loads[4:]:
                load.wait()
            loaded = True
        if step == "P":
            stage_p()
        elif step[0] == "N":
            stage_n("fb".index(step[1]))
        elif step[0] in "IO":
            stage_t("fb".index(step[1]), inner if step[0] == "I" else outer)
        elif step[0] == "G":
            stage_g(int(step[1]))
        else:
            t, c = "fb".index(step[1]), "NMAB".index(step[2])
            if step[0] == "S":
                stage_s(c - 2, t, int(step[3]))
            elif step[0] == "U":
                stage_u(c - 2, t, int(step[3]))
            else:
                stages[step[0]](c, t)

    outs = (mixed_o, tgrad_o)
    for t in range(2):
        for h in range(2):
            remote(
                rsum.at[0, t, :, parts[h]], fback.at[t, :, parts[h]], u_ss.at[0, t, h],
                fb_rs.at[t, h], at(far_z[0], my_x),
            ).wait_recv()
            outs[t][:, spans[h]] = (
                nsum[t, :, spans[h]] + fback[t, :, spans[h]].astype(F32)
            ).astype(BF)

    send_meta().wait_send()
    for t in range(2):
        for h in range(2):
            send_block(t, h).wait_send()
            for r in range(2):
                pass_on(r, 1, t, h).wait_send()
        for j in range(3):
            send_near(j, t).wait_send()
        for c in range(CHUNKS):
            for copy in (rs1(c, t), rs2(c, t), ag_y(c, t), ag_m(c, t), ag_r(c, t)):
                copy.wait_send()
        for c, j in ((0, 1), (1, 0), (1, 1)):
            give(c, j, t).wait_send()

    pieces = [(r, t, h) for r in range(2) for t in range(2) for h in range(2)]

    @pl.when(inner)
    def _():
        for r, t, h in pieces:
            for j in range(3):
                send_relay(r, j, t, h).wait_send()
            send_sum(r, t, h).wait_send()

    @pl.when(outer)
    def _():
        for r, t, h in pieces:
            pass_on(r, 0, t, h).wait_send()

    for q in range(4):
        store(q).wait()


def finish_kernel(mixed_r, tgrad_r, dg_h, mixed_o, tgrad_o, dg_o, sem):
    part = dg_h.shape[0] // CHUNKS
    spans = [pl.ds(i * part, part) for i in range(CHUNKS)]
    outs = [pltpu.make_async_copy(dg_h.at[s], dg_o.at[s], sem.at[i]) for i, s in enumerate(spans)]
    for copy in outs:
        copy.start()
    mixed_o[...] = mixed_r[...]
    tgrad_o[...] = tgrad_r[...]
    for copy in outs:
        copy.wait()


def fused(tokens, expert_ids, gates, cotangent, w_gate, w_up, w_down):
    n_tok, topk = expert_ids.shape
    cols = tokens.shape[1]
    hid = w_gate.shape[2]
    n_exp, n_sec = lax.axis_size("expert"), lax.axis_size("section")
    cap = capacity_of(n_tok, topk, n_exp)
    quarter = hid // n_sec
    group = n_exp // 2
    vm = pl.BlockSpec(memory_space=pltpu.VMEM)
    hbm = pl.BlockSpec(memory_space=pl.ANY)
    dma = pltpu.SemaphoreType.DMA
    ids_r, gate_r = expert_ids.T, gates.T
    shapes = (
        jax.ShapeDtypeStruct((n_tok, cols), BF),
        jax.ShapeDtypeStruct((n_tok, cols), BF),
        jax.ShapeDtypeStruct((hid, cols), BF),
    )

    def per(j, *lead):
        return pltpu.VMEM((n_exp, *lead, j, cap, quarter), BF)

    results = pl.pallas_call(
        functools.partial(expert_kernel, n_exp, cap),
        out_shape=shapes,
        in_specs=[pl.BlockSpec(memory_space=pltpu.HBM)] * 7,
        out_specs=(vm, vm, hbm),
        scratch_shapes=[
            pltpu.VMEM((topk, n_tok), jnp.int32),
            pltpu.VMEM((topk, n_tok), F32),
            pltpu.VMEM((n_tok, cols), BF),
            pltpu.VMEM((n_tok, cols), BF),
            pltpu.VMEM((cols, hid), BF),
            pltpu.VMEM((cols, hid), BF),
            pltpu.VMEM((hid, cols), BF),
            pltpu.VMEM((8, n_tok), F32),
            pltpu.VMEM((2, 8, n_tok), F32),
            pltpu.VMEM((3, group * cap, n_tok), BF),
            pltpu.VMEM((3, group * cap, n_tok), BF),
            pltpu.VMEM((3, group * cap, n_tok), BF),
            pltpu.VMEM((3, group * cap, 1), F32),
            pltpu.VMEM((2, group, cap, cols), BF),
            pltpu.VMEM((CHUNKS, 2, 2, cap, cols), BF),
            pltpu.VMEM((2, 2, n_tok, cols), BF),
            pltpu.VMEM((2, 2, group, cap, cols), BF),
            per(2, 2, 2), per(1, 2, 2), per(2, 2), per(1, 2), per(2), per(1), per(2), per(1),
            per(1, 2, 2), per(2, 2, 2),
            pltpu.VMEM((n_exp, cap, quarter), F32),
            pltpu.VMEM((n_exp, cap, quarter), F32),
            pltpu.VMEM((CHUNKS, 2, cap, hid), BF),
            pltpu.VMEM((CHUNKS, 2, 2, cap, cols), BF),
            pltpu.VMEM((2, group, cap, cols), BF),
            pltpu.VMEM((2, 2, group, cap, cols), BF),
            pltpu.VMEM((2, 2, n_tok, cols), BF),
            pltpu.VMEM((2, n_tok, cols), BF),
            pltpu.VMEM((2, n_tok, cols), F32),
            pltpu.VMEM((hid, cols), BF),
            dma((7,)), dma, dma((2,)), dma((3, 2)), dma((2, 2, 2)), dma((2, 2)),
            dma((2, 2, 2)), dma((2, 3, 2, 2)), dma((2, 2, 2, 2)),
        ]
        + [dma((2 * CHUNKS,)) for _ in range(10)]
        + [
            dma((2, 2, 2)), dma((2, 2, 2, 2)), dma((group, 2)), dma((2, group, 2, 2)),
            dma((2, 2, 2)), dma((2, 2)), dma((4,)),
        ],
        compiler_params=pltpu.CompilerParams(
            collective_id=0, has_side_effects=True, vmem_limit_bytes=40 * 1024 * 1024
        ),
    )(
        *[
            pltpu.with_memory_space_constraint(x, pltpu.HBM)
            for x in (ids_r, gate_r, tokens, cotangent, w_gate[0], w_up[0], w_down[0])
        ]
    )
    mixed, tgrad, dg = pl.pallas_call(
        finish_kernel,
        out_shape=shapes,
        in_specs=[vm, vm, hbm],
        out_specs=(vm, vm, hbm),
        scratch_shapes=[dma((CHUNKS,))],
        compiler_params=pltpu.CompilerParams(vmem_limit_bytes=8 * 1024 * 1024),
    )(*results)
    return mixed, tgrad, dg[None]


def capacity_of(tok_rows, top_count, expert_count):
    return min(tok_rows, max(2, 3 * tok_rows * top_count // (2 * expert_count)))


def layer(tokens, expert_ids, *rest):
    n_exp, n_sec = lax.axis_size("expert"), lax.axis_size("section")
    n_tok, topk = expert_ids.shape
    cap = capacity_of(n_tok, topk, n_exp)
    hid = rest[2].shape[2]
    tiles = (
        n_exp == 2 * CHUNKS and n_sec == 4 and cap % 16 == 0 and n_tok % 128 == 0
        and tokens.shape[1] % 128 == 0 and hid % (n_sec * 128) == 0
    )
    return (fused if tiles else local)(tokens, expert_ids, *rest)


def solution(mesh):
    placed = (
        P("expert", "section"),
        P("expert", None),
        P("expert", None),
        P("expert", "section"),
        P("expert", "section", None),
        P("expert", "section", None),
        P("expert", None, "section"),
    )
    return jax.shard_map(
        layer,
        mesh=mesh,
        in_specs=placed,
        out_specs=(P("expert", "section"), P("expert", "section"), P("expert", None, "section")),
        check_vma=False,
    )
```

```python
import functools

import jax
import jax.numpy as jnp
from jax import lax
from jax.experimental import pallas as pl
from jax.experimental.pallas import tpu as pltpu
from jax.sharding import PartitionSpec as P


def local(tokens, expert_ids, gates, cotangent, w_gate, w_up, w_down):
    tok_rows, top_count = expert_ids.shape
    col_span = tokens.shape[1]
    expert_count = lax.axis_size("expert")
    capacity = capacity_of(tok_rows, top_count, expert_count)
    slot_total = expert_count * capacity
    one_hot = (
        expert_ids[:, :, None] == jnp.arange(expert_count, dtype=jnp.int32)[None, None, :]
    ).astype(jnp.int32)
    one_hot = one_hot.reshape(tok_rows * top_count, expert_count)
    pairs = jnp.arange(tok_rows * top_count, dtype=jnp.int32)
    earlier = jnp.dot(
        (pairs[None, :] < pairs[:, None]).astype(jnp.bfloat16),
        one_hot.astype(jnp.bfloat16),
        preferred_element_type=jnp.float32,
    ).astype(jnp.int32)
    ranks = jnp.sum(earlier * one_hot, axis=1)
    slot_ids = expert_ids.reshape(-1) * capacity + ranks
    picker = (slot_ids[:, None] == jnp.arange(slot_total, dtype=jnp.int32)[None, :]).astype(
        jnp.float32
    )
    picker_rows = picker.reshape(tok_rows, top_count, slot_total)
    chooser = jnp.sum(picker_rows, axis=1)
    weigher = jnp.sum(picker_rows * gates[:, :, None], axis=1)
    sent_rows = jnp.dot(
        chooser.T.astype(jnp.bfloat16), tokens, preferred_element_type=jnp.float32
    ).astype(jnp.bfloat16)
    sent_grads = jnp.dot(
        weigher.T, cotangent.astype(jnp.float32), precision=lax.Precision.HIGHEST
    ).astype(jnp.bfloat16)
    routed_rows, routed_grads = (
        lax.all_to_all(sent_rows, "expert", split_axis=0, concat_axis=0, tiled=True),
        lax.all_to_all(sent_grads, "expert", split_axis=0, concat_axis=0, tiled=True),
    )
    gate_w = w_gate[0]
    up_w = w_up[0]
    down_w = w_down[0]
    grad_term = jnp.einsum("rc,hc->rh", routed_grads, down_w, preferred_element_type=jnp.float32)
    gate_term = jnp.dot(routed_rows, gate_w, preferred_element_type=jnp.float32)
    up_term = jnp.dot(routed_rows, up_w, preferred_element_type=jnp.float32)
    gate_pre, up_pre, hidden_grad = (
        lax.psum_scatter(
            gate_term.astype(jnp.bfloat16), "section", scatter_dimension=1, tiled=True
        ).astype(jnp.float32),
        lax.psum_scatter(
            up_term.astype(jnp.bfloat16), "section", scatter_dimension=1, tiled=True
        ).astype(jnp.float32),
        lax.psum_scatter(
            grad_term.astype(jnp.bfloat16), "section", scatter_dimension=1, tiled=True
        ).astype(jnp.float32),
    )
    sigmoid_val = jax.nn.sigmoid(gate_pre)
    activated = gate_pre * sigmoid_val
    hidden = (activated * up_pre).astype(jnp.bfloat16)
    gate_grad = (
        hidden_grad * up_pre * sigmoid_val * (1.0 + gate_pre * (1.0 - sigmoid_val))
    ).astype(jnp.bfloat16)
    up_grad = (hidden_grad * activated).astype(jnp.bfloat16)
    full_hidden, full_gate_grad, full_up_grad = (
        lax.all_gather(hidden, "section", axis=1, tiled=True),
        lax.all_gather(gate_grad, "section", axis=1, tiled=True),
        lax.all_gather(up_grad, "section", axis=1, tiled=True),
    )
    out_rows = jnp.dot(full_hidden, down_w, preferred_element_type=jnp.float32).astype(jnp.bfloat16)
    down_grad = jnp.einsum(
        "rh,rc->hc", full_hidden, routed_grads, preferred_element_type=jnp.float32
    ).astype(jnp.bfloat16)
    slot_grad = jnp.einsum("rh,ch->rc", full_gate_grad, gate_w, preferred_element_type=jnp.float32)
    slot_grad = (
        slot_grad + jnp.einsum("rh,ch->rc", full_up_grad, up_w, preferred_element_type=jnp.float32)
    ).astype(jnp.bfloat16)
    back_out, back_grad = (
        lax.all_to_all(out_rows, "expert", split_axis=0, concat_axis=0, tiled=True),
        lax.all_to_all(slot_grad, "expert", split_axis=0, concat_axis=0, tiled=True),
    )
    picked_out = jnp.dot(picker.astype(jnp.bfloat16), back_out, preferred_element_type=jnp.float32)
    picked_out = picked_out.reshape(tok_rows, top_count, col_span)
    mixed = jnp.sum(gates[:, :, None] * picked_out, axis=1).astype(jnp.bfloat16)
    token_grads = jnp.dot(
        chooser.astype(jnp.bfloat16), back_grad, preferred_element_type=jnp.float32
    ).astype(jnp.bfloat16)
    return (mixed, token_grads, down_grad[None])


MESH = pl.DeviceIdType.MESH
CHUNKS = 4
NEAR = "NM"
NT = (((1,), (1,)), ((), ()))
TN = (((0,), (0,)), ((), ()))
F32 = jnp.float32
BF = jnp.bfloat16
STEPS = (
    "If", "Nf", "Nb", "Ib", "SfA0", "AfM", "BfM", "AfN", "SfA1", "AbN",
    "Of", "AbM", "BfN", "Ob", "SbA0", "CfM", "BbM", "SbA1", "BbN", "AfA",
    "SfB0", "BfA", "DfM", "CfN", "AbA", "SfB1", "BbA", "SbB0", "CfA", "EfM",
    "CbA", "AfB", "DfA", "BfB", "SbB1", "EfA", "CbM", "DbA", "EbA", "CfB",
    "AbB", "UfA0", "DbM", "BbB", "DfB", "DfN", "UfA1", "CbN", "EfB", "UbA0",
    "EbM", "CbB", "EfN", "G0", "UbA1", "G3", "G2", "DbN", "UfB0", "DbB",
    "EbB", "UfB1", "EbN", "UbB0", "UbB1", "G1", "P",
)


def expert_kernel(
    n_exp, cap, ids_h, gate_h, tok_h, cot_h, wg_h, wu_h, wd_h,
    mixed_o, tgrad_o, dg_o,
    ids_r, gate_r, tok, cot, wg, wu, wd, meta, metas, pick, whi, wlo, gcol, nsend, recv, tbuf, rsend,
    part_f, part_b, r1_f, r1_b, s2_f, s2_b, r2_f, r2_b, act_f, act_b, slope, silu_s,
    hbuf, obuf, bnear, rback, rsum, fback, nsum, dgbuf,
    w_sem, meta_ss, meta_rs, n_ss, d_rs, t_ss, t_rs, rl_ss, dx_rs,
    s1_ss, s1_rs, s2_ss, s2_rs, gy_ss, gy_rs, gm_ss, gm_rs, gr_ss, gr_rs,
    b_ss, bx_ss, bn_rs, rb_rs, u_ss, fb_rs, o_sem,
):
    me_e = lax.axis_index("expert")
    me_s = lax.axis_index("section")
    my_z, my_x = me_e // 2, me_e % 2
    oth_z, oth_x = my_z + 1 - 2 * (my_z % 2), 1 - my_x
    side = my_z // 2
    inner = my_z == 1 + side
    far_z = (2 - side, 3 - 3 * side)
    rank_in = (my_z + side + 1) % 2
    first = 4 * side
    my_y, my_c = me_s // 2, me_s % 2
    oth_y, oth_c = 1 - my_y, 1 - my_c
    mate = my_y * 2 + oth_c
    ypart = oth_y * 2 + my_c
    n_tok, cols = tok.shape
    hid = wg.shape[1]
    quarter = hid // 4
    topk = ids_r.shape[0]
    half = (n_exp // 2) * cap
    cut = (cols // 128 + 1) // 2 * 128
    spans = (slice(0, cut), slice(cut, cols))
    parts = (pl.ds(0, cut), pl.ds(cut, cols - cut))

    my_l = (my_z % 2) * 2 + my_x
    near = ((my_z, oth_x), (oth_z, my_x), (oth_z, oth_x))
    near_l = [(z % 2) * 2 + x for z, x in near]

    def at(z, x):
        return (me_s, z * 2 + x)

    def remote(src, dst, ss, rs, dev):
        return pltpu.make_async_remote_copy(
            src_ref=src, dst_ref=dst, send_sem=ss, recv_sem=rs, device_id=dev,
            device_id_type=MESH,
        )

    outer = jnp.logical_not(inner)
    barrier = pltpu.get_barrier_semaphore()
    friends = [at(far_z[0], my_x)] + [at(z, x) for z, x in near[::-1]]
    friends += [(ypart, me_e), (mate, me_e)]

    @pl.when(inner)
    def _():
        pl.semaphore_signal(
            barrier, inc=1, device_id=at(far_z[1], my_x), device_id_type=MESH
        )

    for dev in friends:
        pl.semaphore_signal(barrier, inc=1, device_id=dev, device_id_type=MESH)

    moves = (
        (ids_h, ids_r), (gate_h, gate_r), (tok_h, tok), (cot_h, cot),
        (wg_h, wg), (wu_h, wu), (wd_h, wd),
    )
    loads = [pltpu.make_async_copy(a, b, w_sem.at[i]) for i, (a, b) in enumerate(moves)]
    for load in loads:
        load.start()

    e_r = lax.broadcasted_iota(jnp.int32, (n_exp, n_tok), 0).astype(F32)
    t0 = lax.broadcasted_iota(jnp.int32, (n_tok, n_tok), 0)
    t1 = lax.broadcasted_iota(jnp.int32, (n_tok, n_tok), 1)
    before = (t0 < t1).astype(BF)
    s_iota = lax.broadcasted_iota(jnp.int32, (half, n_tok), 0)

    def prepare(i, ids, gates):
        hot = [(ids[k : k + 1, :] == e_r).astype(F32) for k in range(topk)]
        base = jnp.dot(sum(hot).astype(BF), before, preferred_element_type=F32) + e_r * cap
        chosen = jnp.zeros((half, n_tok), F32)
        weight = jnp.zeros((half, n_tok), F32)
        for k in range(topk):
            slot = jnp.sum(hot[k] * base, axis=0, keepdims=True).astype(jnp.int32)
            hit = (slot - first * cap == s_iota).astype(F32)
            chosen = chosen + hit
            weight = weight + hit * gates[k : k + 1, :]
            base = base + hot[k]
        pick[i] = chosen.astype(BF)
        high = weight.astype(BF)
        whi[i] = high
        wlo[i] = (weight - high.astype(F32)).astype(BF)
        gcol[i] = jnp.sum(weight, axis=1, keepdims=True)

    def select(i, t, rows):
        got = jnp.dot(pick[i], rows, preferred_element_type=F32)
        if t:
            got = got * gcol[i]
        return got.astype(BF).reshape(n_exp // 2, cap, rows.shape[-1])

    def collect(i, t, rows):
        rows = rows.reshape(half, rows.shape[-1])
        if t:
            return lax.dot_general(pick[i], rows, TN, preferred_element_type=F32)
        return lax.dot_general(whi[i], rows, TN, preferred_element_type=F32) + lax.dot_general(
            wlo[i], rows, TN, preferred_element_type=F32
        )

    def send_meta():
        return remote(
            meta, metas.at[rank_in], meta_ss, meta_rs.at[rank_in], at(far_z[0], my_x)
        )

    def send_block(t, h):
        return remote(
            (tok, cot)[t].at[:, parts[h]], tbuf.at[rank_in, t, :, parts[h]], t_ss.at[t, h],
            t_rs.at[rank_in, t, h], at(far_z[0], my_x),
        )

    def send_near(j, t):
        c = 1 if j else 0
        return remote(
            nsend.at[t, near_l[j]], recv.at[c, my_x, t], n_ss.at[j, t], d_rs.at[c, my_x, t],
            at(*near[j]),
        )

    def send_relay(r, j, t, h):
        return remote(
            rsend.at[r, t, near_l[j], :, parts[h]], recv.at[2 + r, my_x, t, :, parts[h]],
            rl_ss.at[r, j, t, h], dx_rs.at[r, my_x, t, h], at(*near[j]),
        )

    def relayed(r, x, t, h):
        return remote(
            rsend.at[r, t, 0, :, parts[h]], recv.at[2 + r, x, t, :, parts[h]],
            rl_ss.at[r, 0, t, h], dx_rs.at[r, x, t, h], at(*near[0]),
        )

    def arrived(c, x, t):
        return remote(
            nsend.at[t, 0], recv.at[c, x, t], n_ss.at[0, t], d_rs.at[c, x, t], at(*near[0])
        )

    def give(c, j, t):
        x = oth_x if j else my_x
        return remote(
            obuf.at[c, x, t], bnear.at[t, my_l], b_ss.at[c, j, t], bn_rs.at[my_l, t],
            at(oth_z if c else my_z, x),
        )

    def pass_on(r, j, t, h):
        x = oth_x if j else my_x
        return remote(
            obuf.at[2 + r, x, t, :, parts[h]], rback.at[r, t, my_l, :, parts[h]],
            bx_ss.at[r, j, t, h], rb_rs.at[r, my_l, t, h], at(1 + side, x),
        )

    def send_sum(r, t, h):
        return remote(
            rsum.at[r, t, :, parts[h]], fback.at[t, :, parts[h]], u_ss.at[r, t, h],
            fb_rs.at[t, h], at(far_z[r], my_x),
        )

    def to_section(src, dst, ss, rs, s):
        return remote(src, dst, ss, rs, (s, me_e))

    part, r1, s2, r2 = (part_f, part_b), (r1_f, r1_b), (s2_f, s2_b), (r2_f, r2_b)
    act = (act_f, act_b)

    def pair(c):
        return pl.ds(2 * c, 2)

    def rs1(c, t):
        k = 2 * c + t
        return to_section(
            part[t].at[pair(c), oth_c], r1[t].at[pair(c)], s1_ss.at[k], s1_rs.at[k], mate
        )

    def rs2(c, t):
        k = 2 * c + t
        return to_section(s2[t].at[pair(c)], r2[t].at[pair(c)], s2_ss.at[k], s2_rs.at[k], ypart)

    def ag_y(c, t, y=None):
        k = 2 * c + t
        mine = act[t].at[pair(c), my_c, my_y if y is None else y]
        return to_section(mine, mine, gy_ss.at[k], gy_rs.at[k], ypart)

    def ag_m(c, t, core=None):
        k = 2 * c + t
        mine = act[t].at[pair(c), my_c if core is None else core, my_y]
        return to_section(mine, mine, gm_ss.at[k], gm_rs.at[k], mate)

    def ag_r(c, t, core=None):
        k = 2 * c + t
        mine = act[t].at[pair(c), my_c if core is None else core, oth_y]
        return to_section(mine, mine, gr_ss.at[k], gr_rs.at[k], mate)

    def near_step(t):
        picked = select(0, t, (tok, cot)[t][...])
        nsend[t] = picked
        recv[0, my_x, t] = nsend[t, my_l]

    def stage_s(r, t, h):
        @pl.when(inner)
        def _():
            if not t and not h:
                remote(
                    meta, metas.at[r], meta_ss, meta_rs.at[r], at(far_z[0], my_x)
                ).wait_recv()
                prepare(1 + r, metas[r, 0:topk, :], metas[r, topk : 2 * topk, :])
            remote(
                tok.at[:, parts[h]], tbuf.at[r, t, :, parts[h]], t_ss.at[t, h],
                t_rs.at[r, t, h], at(far_z[0], my_x),
            ).wait_recv()
            rsend[r, t, :, :, spans[h]] = select(1 + r, t, tbuf[r, t, :, spans[h]])
            for j in (2, 1, 0):
                send_relay(r, j, t, h).start()
            recv[2 + r, my_x, t, :, spans[h]] = rsend[r, t, my_l, :, spans[h]]

    def stage_a(c, t):
        if c < 2:
            arrived(c, oth_x, t).wait_recv()
            if c == 1:
                arrived(c, my_x, t).wait_recv()
        else:
            for h in range(2):
                relayed(c - 2, oth_x, t, h).wait_recv()

            @pl.when(outer)
            def _():
                for h in range(2):
                    relayed(c - 2, my_x, t, h).wait_recv()

        x = recv[c, :, t].reshape(2 * cap, cols)
        for q in range(4):
            span = slice(q * quarter, (q + 1) * quarter)
            if t:
                terms = [lax.dot_general(x, wd[span, :], NT, preferred_element_type=F32)]
            else:
                terms = [jnp.dot(x, w[:, span], preferred_element_type=F32) for w in (wg, wu)]
            for j, term in enumerate(terms):
                part[t][pair(c), q // 2, q % 2, j] = term.astype(BF).reshape(2, cap, quarter)
        rs1(c, t).start()

    def stage_b(c, t):
        b = pair(c)
        rs1(c, t).wait_recv()
        s2[t][b] = (part[t][b, my_c, oth_y].astype(F32) + r1[t][b, oth_y].astype(F32)).astype(BF)
        rs2(c, t).start()

    def stage_c(c, t):
        b = pair(c)
        rs2(c, t).wait_recv()

        def total(j):
            return (
                part[t][b, my_c, my_y, j].astype(F32) + r1[t][b, my_y, j].astype(F32)
                + r2[t][b, j].astype(F32)
            )

        if t:
            hg = total(0)
            act_b[b, my_c, my_y, 0] = (hg * slope[b]).astype(BF)
            act_b[b, my_c, my_y, 1] = (hg * silu_s[b]).astype(BF)
        else:
            pre, up = total(0), total(1)
            sig = jax.nn.sigmoid(pre)
            silu = pre * sig
            act_f[b, my_c, my_y, 0] = (silu * up).astype(BF)
            slope[b] = up * sig * (1.0 + pre * (1.0 - sig))
            silu_s[b] = silu
        ag_y(c, t).start()
        ag_m(c, t).start()

    def stage_d(c, t):
        ag_y(c, t, oth_y).wait_recv()
        ag_r(c, t).start()

    def stage_e(c, t):
        ag_m(c, t, oth_c).wait_recv()
        ag_r(c, t, oth_c).wait_recv()
        full = [
            jnp.concatenate(
                [act[t][pair(c), q // 2, q % 2, j].reshape(2 * cap, quarter) for q in range(4)],
                axis=1,
            )
            for j in range(1 + t)
        ]
        if not t:
            hbuf[c] = full[0].reshape(2, cap, hid)

        def product(span):
            if t:
                out = lax.dot_general(full[0], wg[span, :], NT, preferred_element_type=F32)
                out = out + lax.dot_general(
                    full[1], wu[span, :], NT, preferred_element_type=F32
                )
            else:
                out = jnp.dot(full[0], wd[:, span], preferred_element_type=F32)
            return out.astype(BF).reshape(2, cap, out.shape[-1])

        if c < 2:
            obuf[c, :, t] = product(slice(0, cols))
            give(c, 1, t).start()
            if c:
                give(c, 0, t).start()
            else:
                bnear[t, my_l] = obuf[c, my_x, t]
            return
        for h in range(2):
            obuf[c, :, t, :, spans[h]] = product(spans[h])
            pass_on(c - 2, 1, t, h).start()

            @pl.when(inner)
            def _(h=h):
                rback[c - 2, t, my_l, :, spans[h]] = obuf[c, my_x, t, :, spans[h]]

            @pl.when(outer)
            def _(h=h):
                pass_on(c - 2, 0, t, h).start()

    def stage_u(r, t, h):
        @pl.when(inner)
        def _():
            for ld in near_l:
                remote(
                    obuf.at[2, 0, t, :, parts[h]], rback.at[r, t, ld, :, parts[h]],
                    bx_ss.at[0, 1, t, h], rb_rs.at[r, ld, t, h], at(*near[0]),
                ).wait_recv()
            rsum[r, t, :, spans[h]] = collect(1 + r, t, rback[r, t, :, :, spans[h]]).astype(BF)
            send_sum(r, t, h).start()

    def stage_g(q):
        span = slice(q * quarter, (q + 1) * quarter)
        all_g = recv[:, :, 1].reshape(n_exp * cap, cols)
        hq = hbuf[:, :, :, span].reshape(n_exp * cap, quarter)
        dgbuf[span, :] = lax.dot_general(hq, all_g, TN, preferred_element_type=F32).astype(BF)
        store(q).start()

    def store(q):
        span = pl.ds(q * quarter, quarter)
        return pltpu.make_async_copy(dgbuf.at[span], dg_o.at[span], o_sem.at[q])

    def stage_p():
        for t in range(2):
            for ld in near_l:
                remote(
                    obuf.at[0, 0, t], bnear.at[t, ld], b_ss.at[0, 1, t], bn_rs.at[ld, t],
                    at(*near[0]),
                ).wait_recv()
            nsum[t] = collect(0, t, bnear[t])

    for load in loads[:4]:
        load.wait()
    meta[...] = jnp.concatenate(
        [ids_r[...].astype(F32), gate_r[...], jnp.zeros((8 - 2 * topk, n_tok), F32)], axis=0
    )
    prepare(0, ids_r[...].astype(F32), gate_r[...])
    near_step(0)
    @pl.when(inner)
    def _():
        pl.semaphore_wait(barrier, len(friends) + 1)

    @pl.when(outer)
    def _():
        pl.semaphore_wait(barrier, len(friends))

    send_meta().start()

    def stage_n(t):
        if t:
            near_step(t)
        for j in (2, 1, 0):
            send_near(j, t).start()

    def stage_t(t, role):
        @pl.when(role)
        def _():
            for h in range(2):
                send_block(t, h).start()

    stages = {
        "A": stage_a, "B": stage_b, "C": stage_c, "D": stage_d, "E": stage_e,
    }
    loaded = False
    for step in STEPS:
        if step[0] == "A" and not loaded:
            for load in loads[4:]:
                load.wait()
            loaded = True
        if step == "P":
            stage_p()
        elif step[0] == "N":
            stage_n("fb".index(step[1]))
        elif step[0] in "IO":
            stage_t("fb".index(step[1]), inner if step[0] == "I" else outer)
        elif step[0] == "G":
            stage_g(int(step[1]))
        else:
            t, c = "fb".index(step[1]), "NMAB".index(step[2])
            if step[0] == "S":
                stage_s(c - 2, t, int(step[3]))
            elif step[0] == "U":
                stage_u(c - 2, t, int(step[3]))
            else:
                stages[step[0]](c, t)

    outs = (mixed_o, tgrad_o)
    for t in range(2):
        for h in range(2):
            remote(
                rsum.at[0, t, :, parts[h]], fback.at[t, :, parts[h]], u_ss.at[0, t, h],
                fb_rs.at[t, h], at(far_z[0], my_x),
            ).wait_recv()
            outs[t][:, spans[h]] = (
                nsum[t, :, spans[h]] + fback[t, :, spans[h]].astype(F32)
            ).astype(BF)

    send_meta().wait_send()
    for t in range(2):
        for h in range(2):
            send_block(t, h).wait_send()
            for r in range(2):
                pass_on(r, 1, t, h).wait_send()
        for j in range(3):
            send_near(j, t).wait_send()
        for c in range(CHUNKS):
            for copy in (rs1(c, t), rs2(c, t), ag_y(c, t), ag_m(c, t), ag_r(c, t)):
                copy.wait_send()
        for c, j in ((0, 1), (1, 0), (1, 1)):
            give(c, j, t).wait_send()

    pieces = [(r, t, h) for r in range(2) for t in range(2) for h in range(2)]

    @pl.when(inner)
    def _():
        for r, t, h in pieces:
            for j in range(3):
                send_relay(r, j, t, h).wait_send()
            send_sum(r, t, h).wait_send()

    @pl.when(outer)
    def _():
        for r, t, h in pieces:
            pass_on(r, 0, t, h).wait_send()

    for q in range(4):
        store(q).wait()


def finish_kernel(mixed_r, tgrad_r, dg_r, mixed_o, tgrad_o, dg_o, sem):
    part = dg_r.shape[0] // CHUNKS
    spans = [pl.ds(i * part, part) for i in range(CHUNKS)]
    pairs = [(mixed_r, mixed_o), (tgrad_r, tgrad_o)]
    pairs += [(dg_r.at[span], dg_o.at[span]) for span in spans]
    copies = [pltpu.make_async_copy(a, b, sem.at[i]) for i, (a, b) in enumerate(pairs)]
    for copy in copies:
        copy.start()
    for copy in copies:
        copy.wait()


def fused(tokens, expert_ids, gates, cotangent, w_gate, w_up, w_down):
    n_tok, topk = expert_ids.shape
    cols = tokens.shape[1]
    hid = w_gate.shape[2]
    n_exp, n_sec = lax.axis_size("expert"), lax.axis_size("section")
    cap = capacity_of(n_tok, topk, n_exp)
    quarter = hid // n_sec
    group = n_exp // 2
    vm = pl.BlockSpec(memory_space=pltpu.VMEM)
    hbm = pl.BlockSpec(memory_space=pl.ANY)
    dma = pltpu.SemaphoreType.DMA
    ids_r, gate_r = expert_ids.T, gates.T
    shapes = (
        jax.ShapeDtypeStruct((n_tok, cols), BF),
        jax.ShapeDtypeStruct((n_tok, cols), BF),
        jax.ShapeDtypeStruct((hid, cols), BF),
    )

    def per(j, *lead):
        return pltpu.VMEM((n_exp, *lead, j, cap, quarter), BF)

    results = pl.pallas_call(
        functools.partial(expert_kernel, n_exp, cap),
        out_shape=shapes,
        in_specs=[pl.BlockSpec(memory_space=pltpu.HBM)] * 7,
        out_specs=(vm, vm, hbm),
        scratch_shapes=[
            pltpu.VMEM((topk, n_tok), jnp.int32),
            pltpu.VMEM((topk, n_tok), F32),
            pltpu.VMEM((n_tok, cols), BF),
            pltpu.VMEM((n_tok, cols), BF),
            pltpu.VMEM((cols, hid), BF),
            pltpu.VMEM((cols, hid), BF),
            pltpu.VMEM((hid, cols), BF),
            pltpu.VMEM((8, n_tok), F32),
            pltpu.VMEM((2, 8, n_tok), F32),
            pltpu.VMEM((3, group * cap, n_tok), BF),
            pltpu.VMEM((3, group * cap, n_tok), BF),
            pltpu.VMEM((3, group * cap, n_tok), BF),
            pltpu.VMEM((3, group * cap, 1), F32),
            pltpu.VMEM((2, group, cap, cols), BF),
            pltpu.VMEM((CHUNKS, 2, 2, cap, cols), BF),
            pltpu.VMEM((2, 2, n_tok, cols), BF),
            pltpu.VMEM((2, 2, group, cap, cols), BF),
            per(2, 2, 2), per(1, 2, 2), per(2, 2), per(1, 2), per(2), per(1), per(2), per(1),
            per(1, 2, 2), per(2, 2, 2),
            pltpu.VMEM((n_exp, cap, quarter), F32),
            pltpu.VMEM((n_exp, cap, quarter), F32),
            pltpu.VMEM((CHUNKS, 2, cap, hid), BF),
            pltpu.VMEM((CHUNKS, 2, 2, cap, cols), BF),
            pltpu.VMEM((2, group, cap, cols), BF),
            pltpu.VMEM((2, 2, group, cap, cols), BF),
            pltpu.VMEM((2, 2, n_tok, cols), BF),
            pltpu.VMEM((2, n_tok, cols), BF),
            pltpu.VMEM((2, n_tok, cols), F32),
            pltpu.VMEM((hid, cols), BF),
            dma((7,)), dma, dma((2,)), dma((3, 2)), dma((2, 2, 2)), dma((2, 2)),
            dma((2, 2, 2)), dma((2, 3, 2, 2)), dma((2, 2, 2, 2)),
        ]
        + [dma((2 * CHUNKS,)) for _ in range(10)]
        + [
            dma((2, 2, 2)), dma((2, 2, 2, 2)), dma((group, 2)), dma((2, group, 2, 2)),
            dma((2, 2, 2)), dma((2, 2)), dma((4,)),
        ],
        compiler_params=pltpu.CompilerParams(
            collective_id=0, has_side_effects=True, vmem_limit_bytes=40 * 1024 * 1024
        ),
    )(
        *[
            pltpu.with_memory_space_constraint(x, pltpu.HBM)
            for x in (ids_r, gate_r, tokens, cotangent, w_gate[0], w_up[0], w_down[0])
        ]
    )
    mixed, tgrad, dg = pl.pallas_call(
        finish_kernel,
        out_shape=shapes,
        in_specs=[hbm] * 3,
        out_specs=(hbm,) * 3,
        scratch_shapes=[dma((CHUNKS + 2,))],
        compiler_params=pltpu.CompilerParams(vmem_limit_bytes=8 * 1024 * 1024),
    )(*results)
    return mixed, tgrad, dg[None]


def capacity_of(tok_rows, top_count, expert_count):
    return min(tok_rows, max(2, 3 * tok_rows * top_count // (2 * expert_count)))


def layer(tokens, expert_ids, *rest):
    n_exp, n_sec = lax.axis_size("expert"), lax.axis_size("section")
    n_tok, topk = expert_ids.shape
    cap = capacity_of(n_tok, topk, n_exp)
    hid = rest[2].shape[2]
    tiles = (
        n_exp == 2 * CHUNKS and n_sec == 4 and cap % 16 == 0 and n_tok % 128 == 0
        and tokens.shape[1] % 128 == 0 and hid % (n_sec * 128) == 0
    )
    return (fused if tiles else local)(tokens, expert_ids, *rest)


def solution(mesh):
    placed = (
        P("expert", "section"),
        P("expert", None),
        P("expert", None),
        P("expert", "section"),
        P("expert", "section", None),
        P("expert", "section", None),
        P("expert", None, "section"),
    )
    return jax.shard_map(
        layer,
        mesh=mesh,
        in_specs=placed,
        out_specs=(P("expert", "section"), P("expert", "section"), P("expert", None, "section")),
        check_vma=False,
    )
```

```python
import functools

import jax
import jax.numpy as jnp
from jax import lax
from jax.experimental import pallas as pl
from jax.experimental.pallas import tpu as pltpu
from jax.sharding import PartitionSpec as P


def local(tokens, expert_ids, gates, cotangent, w_gate, w_up, w_down):
    tok_rows, top_count = expert_ids.shape
    col_span = tokens.shape[1]
    expert_count = lax.axis_size("expert")
    capacity = capacity_of(tok_rows, top_count, expert_count)
    slot_total = expert_count * capacity
    one_hot = (
        expert_ids[:, :, None] == jnp.arange(expert_count, dtype=jnp.int32)[None, None, :]
    ).astype(jnp.int32)
    one_hot = one_hot.reshape(tok_rows * top_count, expert_count)
    pairs = jnp.arange(tok_rows * top_count, dtype=jnp.int32)
    earlier = jnp.dot(
        (pairs[None, :] < pairs[:, None]).astype(jnp.bfloat16),
        one_hot.astype(jnp.bfloat16),
        preferred_element_type=jnp.float32,
    ).astype(jnp.int32)
    ranks = jnp.sum(earlier * one_hot, axis=1)
    slot_ids = expert_ids.reshape(-1) * capacity + ranks
    picker = (slot_ids[:, None] == jnp.arange(slot_total, dtype=jnp.int32)[None, :]).astype(
        jnp.float32
    )
    picker_rows = picker.reshape(tok_rows, top_count, slot_total)
    chooser = jnp.sum(picker_rows, axis=1)
    weigher = jnp.sum(picker_rows * gates[:, :, None], axis=1)
    sent_rows = jnp.dot(
        chooser.T.astype(jnp.bfloat16), tokens, preferred_element_type=jnp.float32
    ).astype(jnp.bfloat16)
    sent_grads = jnp.dot(
        weigher.T, cotangent.astype(jnp.float32), precision=lax.Precision.HIGHEST
    ).astype(jnp.bfloat16)
    routed_rows, routed_grads = (
        lax.all_to_all(sent_rows, "expert", split_axis=0, concat_axis=0, tiled=True),
        lax.all_to_all(sent_grads, "expert", split_axis=0, concat_axis=0, tiled=True),
    )
    gate_w = w_gate[0]
    up_w = w_up[0]
    down_w = w_down[0]
    grad_term = jnp.einsum("rc,hc->rh", routed_grads, down_w, preferred_element_type=jnp.float32)
    gate_term = jnp.dot(routed_rows, gate_w, preferred_element_type=jnp.float32)
    up_term = jnp.dot(routed_rows, up_w, preferred_element_type=jnp.float32)
    gate_pre, up_pre, hidden_grad = (
        lax.psum_scatter(
            gate_term.astype(jnp.bfloat16), "section", scatter_dimension=1, tiled=True
        ).astype(jnp.float32),
        lax.psum_scatter(
            up_term.astype(jnp.bfloat16), "section", scatter_dimension=1, tiled=True
        ).astype(jnp.float32),
        lax.psum_scatter(
            grad_term.astype(jnp.bfloat16), "section", scatter_dimension=1, tiled=True
        ).astype(jnp.float32),
    )
    sigmoid_val = jax.nn.sigmoid(gate_pre)
    activated = gate_pre * sigmoid_val
    hidden = (activated * up_pre).astype(jnp.bfloat16)
    gate_grad = (
        hidden_grad * up_pre * sigmoid_val * (1.0 + gate_pre * (1.0 - sigmoid_val))
    ).astype(jnp.bfloat16)
    up_grad = (hidden_grad * activated).astype(jnp.bfloat16)
    full_hidden, full_gate_grad, full_up_grad = (
        lax.all_gather(hidden, "section", axis=1, tiled=True),
        lax.all_gather(gate_grad, "section", axis=1, tiled=True),
        lax.all_gather(up_grad, "section", axis=1, tiled=True),
    )
    out_rows = jnp.dot(full_hidden, down_w, preferred_element_type=jnp.float32).astype(jnp.bfloat16)
    down_grad = jnp.einsum(
        "rh,rc->hc", full_hidden, routed_grads, preferred_element_type=jnp.float32
    ).astype(jnp.bfloat16)
    slot_grad = jnp.einsum("rh,ch->rc", full_gate_grad, gate_w, preferred_element_type=jnp.float32)
    slot_grad = (
        slot_grad + jnp.einsum("rh,ch->rc", full_up_grad, up_w, preferred_element_type=jnp.float32)
    ).astype(jnp.bfloat16)
    back_out, back_grad = (
        lax.all_to_all(out_rows, "expert", split_axis=0, concat_axis=0, tiled=True),
        lax.all_to_all(slot_grad, "expert", split_axis=0, concat_axis=0, tiled=True),
    )
    picked_out = jnp.dot(picker.astype(jnp.bfloat16), back_out, preferred_element_type=jnp.float32)
    picked_out = picked_out.reshape(tok_rows, top_count, col_span)
    mixed = jnp.sum(gates[:, :, None] * picked_out, axis=1).astype(jnp.bfloat16)
    token_grads = jnp.dot(
        chooser.astype(jnp.bfloat16), back_grad, preferred_element_type=jnp.float32
    ).astype(jnp.bfloat16)
    return (mixed, token_grads, down_grad[None])


MESH = pl.DeviceIdType.MESH
CHUNKS = 4
NEAR = "NM"
NT = (((1,), (1,)), ((), ()))
TN = (((0,), (0,)), ((), ()))
F32 = jnp.float32
BF = jnp.bfloat16
STEPS = (
    "If", "Nf", "Nb", "Ib", "SfA0", "AfM", "BfM", "AfN", "SfA1", "AbN",
    "Of", "AbM", "BfN", "Ob", "SbA0", "CfM", "BbM", "SbA1", "BbN", "AfA",
    "SfB0", "BfA", "DfM", "CfN", "AbA", "SfB1", "BbA", "SbB0", "CfA", "EfM",
    "CbA", "AfB", "DfA", "BfB", "SbB1", "EfA", "CbM", "DbA", "EbA", "CfB",
    "AbB", "UfA0", "UfA1", "DbM", "BbB", "DfB", "DfN", "CbN", "EfB", "UbA0",
    "EbM", "CbB", "EfN", "G0", "UbA1", "G3", "G2", "DbN", "UfB0", "DbB",
    "EbB", "UfB1", "EbN", "UbB0", "UbB1", "G1", "P",
)


def expert_kernel(
    n_exp, cap, ids_h, gate_h, tok_h, cot_h, wg_h, wu_h, wd_h,
    mixed_o, tgrad_o, dg_o,
    ids_r, gate_r, tok, cot, wg, wu, wd, meta, metas, pick, whi, wlo, gcol, nsend, recv, tbuf, rsend,
    part_f, part_b, r1_f, r1_b, s2_f, s2_b, r2_f, r2_b, act_f, act_b, slope, silu_s,
    hbuf, obuf, bnear, rback, rsum, fback, nsum,
    w_sem, meta_ss, meta_rs, n_ss, d_rs, t_ss, t_rs, rl_ss, dx_rs,
    s1_ss, s1_rs, s2_ss, s2_rs, gy_ss, gy_rs, gm_ss, gm_rs, gr_ss, gr_rs,
    b_ss, bx_ss, bn_rs, rb_rs, u_ss, fb_rs,
):
    me_e = lax.axis_index("expert")
    me_s = lax.axis_index("section")
    my_z, my_x = me_e // 2, me_e % 2
    oth_z, oth_x = my_z + 1 - 2 * (my_z % 2), 1 - my_x
    side = my_z // 2
    inner = my_z == 1 + side
    far_z = (2 - side, 3 - 3 * side)
    rank_in = (my_z + side + 1) % 2
    first = 4 * side
    my_y, my_c = me_s // 2, me_s % 2
    oth_y, oth_c = 1 - my_y, 1 - my_c
    mate = my_y * 2 + oth_c
    ypart = oth_y * 2 + my_c
    n_tok, cols = tok.shape
    hid = wg.shape[1]
    quarter = hid // 4
    topk = ids_r.shape[0]
    half = (n_exp // 2) * cap
    cut = (cols // 128 + 1) // 2 * 128
    spans = (slice(0, cut), slice(cut, cols))
    parts = (pl.ds(0, cut), pl.ds(cut, cols - cut))

    my_l = (my_z % 2) * 2 + my_x
    near = ((my_z, oth_x), (oth_z, my_x), (oth_z, oth_x))
    near_l = [(z % 2) * 2 + x for z, x in near]

    def at(z, x):
        return (me_s, z * 2 + x)

    def remote(src, dst, ss, rs, dev):
        return pltpu.make_async_remote_copy(
            src_ref=src, dst_ref=dst, send_sem=ss, recv_sem=rs, device_id=dev,
            device_id_type=MESH,
        )

    outer = jnp.logical_not(inner)
    barrier = pltpu.get_barrier_semaphore()
    friends = [at(far_z[0], my_x)] + [at(z, x) for z, x in near[::-1]]
    friends += [(ypart, me_e), (mate, me_e)]

    @pl.when(inner)
    def _():
        pl.semaphore_signal(
            barrier, inc=1, device_id=at(far_z[1], my_x), device_id_type=MESH
        )

    for dev in friends:
        pl.semaphore_signal(barrier, inc=1, device_id=dev, device_id_type=MESH)

    moves = (
        (ids_h, ids_r), (gate_h, gate_r), (tok_h, tok), (cot_h, cot),
        (wg_h, wg), (wu_h, wu), (wd_h, wd),
    )
    loads = [pltpu.make_async_copy(a, b, w_sem.at[i]) for i, (a, b) in enumerate(moves)]
    for load in loads:
        load.start()

    e_r = lax.broadcasted_iota(jnp.int32, (n_exp, n_tok), 0).astype(F32)
    t0 = lax.broadcasted_iota(jnp.int32, (n_tok, n_tok), 0)
    t1 = lax.broadcasted_iota(jnp.int32, (n_tok, n_tok), 1)
    before = (t0 < t1).astype(BF)
    s_iota = lax.broadcasted_iota(jnp.int32, (half, n_tok), 0)

    def prepare(i, ids, gates):
        hot = [(ids[k : k + 1, :] == e_r).astype(F32) for k in range(topk)]
        base = jnp.dot(sum(hot).astype(BF), before, preferred_element_type=F32) + e_r * cap
        chosen = jnp.zeros((half, n_tok), F32)
        weight = jnp.zeros((half, n_tok), F32)
        for k in range(topk):
            slot = jnp.sum(hot[k] * base, axis=0, keepdims=True).astype(jnp.int32)
            hit = (slot - first * cap == s_iota).astype(F32)
            chosen = chosen + hit
            weight = weight + hit * gates[k : k + 1, :]
            base = base + hot[k]
        pick[i] = chosen.astype(BF)
        high = weight.astype(BF)
        whi[i] = high
        wlo[i] = (weight - high.astype(F32)).astype(BF)
        gcol[i] = jnp.sum(weight, axis=1, keepdims=True)

    def select(i, t, rows):
        got = jnp.dot(pick[i], rows, preferred_element_type=F32)
        if t:
            got = got * gcol[i]
        return got.astype(BF).reshape(n_exp // 2, cap, rows.shape[-1])

    def collect(i, t, rows):
        rows = rows.reshape(half, rows.shape[-1])
        if t:
            return lax.dot_general(pick[i], rows, TN, preferred_element_type=F32)
        return lax.dot_general(whi[i], rows, TN, preferred_element_type=F32) + lax.dot_general(
            wlo[i], rows, TN, preferred_element_type=F32
        )

    def send_meta():
        return remote(
            meta, metas.at[rank_in], meta_ss, meta_rs.at[rank_in], at(far_z[0], my_x)
        )

    def send_block(t, h):
        return remote(
            (tok, cot)[t].at[:, parts[h]], tbuf.at[rank_in, t, :, parts[h]], t_ss.at[t, h],
            t_rs.at[rank_in, t, h], at(far_z[0], my_x),
        )

    def send_near(j, t):
        c = 1 if j else 0
        return remote(
            nsend.at[t, near_l[j]], recv.at[c, my_x, t], n_ss.at[j, t], d_rs.at[c, my_x, t],
            at(*near[j]),
        )

    def send_relay(r, j, t, h):
        return remote(
            rsend.at[r, t, near_l[j], :, parts[h]], recv.at[2 + r, my_x, t, :, parts[h]],
            rl_ss.at[r, j, t, h], dx_rs.at[r, my_x, t, h], at(*near[j]),
        )

    def relayed(r, x, t, h):
        return remote(
            rsend.at[r, t, 0, :, parts[h]], recv.at[2 + r, x, t, :, parts[h]],
            rl_ss.at[r, 0, t, h], dx_rs.at[r, x, t, h], at(*near[0]),
        )

    def arrived(c, x, t):
        return remote(
            nsend.at[t, 0], recv.at[c, x, t], n_ss.at[0, t], d_rs.at[c, x, t], at(*near[0])
        )

    def give(c, j, t):
        x = oth_x if j else my_x
        return remote(
            obuf.at[c, x, t], bnear.at[t, my_l], b_ss.at[c, j, t], bn_rs.at[my_l, t],
            at(oth_z if c else my_z, x),
        )

    def pass_on(r, j, t, h):
        x = oth_x if j else my_x
        return remote(
            obuf.at[2 + r, x, t, :, parts[h]], rback.at[r, t, my_l, :, parts[h]],
            bx_ss.at[r, j, t, h], rb_rs.at[r, my_l, t, h], at(1 + side, x),
        )

    def send_sum(r, t, h):
        return remote(
            rsum.at[r, t, :, parts[h]], fback.at[t, :, parts[h]], u_ss.at[r, t, h],
            fb_rs.at[t, h], at(far_z[r], my_x),
        )

    def to_section(src, dst, ss, rs, s):
        return remote(src, dst, ss, rs, (s, me_e))

    part, r1, s2, r2 = (part_f, part_b), (r1_f, r1_b), (s2_f, s2_b), (r2_f, r2_b)
    act = (act_f, act_b)

    def pair(c):
        return pl.ds(2 * c, 2)

    def rs1(c, t):
        k = 2 * c + t
        return to_section(
            part[t].at[pair(c), oth_c], r1[t].at[pair(c)], s1_ss.at[k], s1_rs.at[k], mate
        )

    def rs2(c, t):
        k = 2 * c + t
        return to_section(s2[t].at[pair(c)], r2[t].at[pair(c)], s2_ss.at[k], s2_rs.at[k], ypart)

    def ag_y(c, t, y=None):
        k = 2 * c + t
        mine = act[t].at[pair(c), my_c, my_y if y is None else y]
        return to_section(mine, mine, gy_ss.at[k], gy_rs.at[k], ypart)

    def ag_m(c, t, core=None):
        k = 2 * c + t
        mine = act[t].at[pair(c), my_c if core is None else core, my_y]
        return to_section(mine, mine, gm_ss.at[k], gm_rs.at[k], mate)

    def ag_r(c, t, core=None):
        k = 2 * c + t
        mine = act[t].at[pair(c), my_c if core is None else core, oth_y]
        return to_section(mine, mine, gr_ss.at[k], gr_rs.at[k], mate)

    def near_step(t):
        picked = select(0, t, (tok, cot)[t][...])
        nsend[t] = picked
        recv[0, my_x, t] = nsend[t, my_l]

    def stage_s(r, t, h):
        @pl.when(inner)
        def _():
            if not t and not h:
                remote(
                    meta, metas.at[r], meta_ss, meta_rs.at[r], at(far_z[0], my_x)
                ).wait_recv()
                prepare(1 + r, metas[r, 0:topk, :], metas[r, topk : 2 * topk, :])
            remote(
                tok.at[:, parts[h]], tbuf.at[r, t, :, parts[h]], t_ss.at[t, h],
                t_rs.at[r, t, h], at(far_z[0], my_x),
            ).wait_recv()
            rsend[r, t, :, :, spans[h]] = select(1 + r, t, tbuf[r, t, :, spans[h]])
            for j in (2, 1, 0):
                send_relay(r, j, t, h).start()
            recv[2 + r, my_x, t, :, spans[h]] = rsend[r, t, my_l, :, spans[h]]

    def stage_a(c, t):
        if c < 2:
            arrived(c, oth_x, t).wait_recv()
            if c == 1:
                arrived(c, my_x, t).wait_recv()
        else:
            for h in range(2):
                relayed(c - 2, oth_x, t, h).wait_recv()

            @pl.when(outer)
            def _():
                for h in range(2):
                    relayed(c - 2, my_x, t, h).wait_recv()

        x = recv[c, :, t].reshape(2 * cap, cols)
        for q in range(4):
            span = slice(q * quarter, (q + 1) * quarter)
            if t:
                terms = [lax.dot_general(x, wd[span, :], NT, preferred_element_type=F32)]
            else:
                terms = [jnp.dot(x, w[:, span], preferred_element_type=F32) for w in (wg, wu)]
            for j, term in enumerate(terms):
                part[t][pair(c), q // 2, q % 2, j] = term.astype(BF).reshape(2, cap, quarter)
        rs1(c, t).start()

    def stage_b(c, t):
        b = pair(c)
        rs1(c, t).wait_recv()
        s2[t][b] = (part[t][b, my_c, oth_y].astype(F32) + r1[t][b, oth_y].astype(F32)).astype(BF)
        rs2(c, t).start()

    def stage_c(c, t):
        b = pair(c)
        rs2(c, t).wait_recv()

        def total(j):
            return (
                part[t][b, my_c, my_y, j].astype(F32) + r1[t][b, my_y, j].astype(F32)
                + r2[t][b, j].astype(F32)
            )

        if t:
            hg = total(0)
            act_b[b, my_c, my_y, 0] = (hg * slope[b]).astype(BF)
            act_b[b, my_c, my_y, 1] = (hg * silu_s[b]).astype(BF)
        else:
            pre, up = total(0), total(1)
            sig = jax.nn.sigmoid(pre)
            silu = pre * sig
            act_f[b, my_c, my_y, 0] = (silu * up).astype(BF)
            slope[b] = up * sig * (1.0 + pre * (1.0 - sig))
            silu_s[b] = silu
        ag_y(c, t).start()
        ag_m(c, t).start()

    def stage_d(c, t):
        ag_y(c, t, oth_y).wait_recv()
        ag_r(c, t).start()

    def stage_e(c, t):
        ag_m(c, t, oth_c).wait_recv()
        ag_r(c, t, oth_c).wait_recv()
        full = [
            jnp.concatenate(
                [act[t][pair(c), q // 2, q % 2, j].reshape(2 * cap, quarter) for q in range(4)],
                axis=1,
            )
            for j in range(1 + t)
        ]
        if not t:
            hbuf[c] = full[0].reshape(2, cap, hid)

        def product(span):
            if t:
                out = lax.dot_general(full[0], wg[span, :], NT, preferred_element_type=F32)
                out = out + lax.dot_general(
                    full[1], wu[span, :], NT, preferred_element_type=F32
                )
            else:
                out = jnp.dot(full[0], wd[:, span], preferred_element_type=F32)
            return out.astype(BF).reshape(2, cap, out.shape[-1])

        if c < 2:
            obuf[c, :, t] = product(slice(0, cols))
            give(c, 1, t).start()
            if c:
                give(c, 0, t).start()
            else:
                bnear[t, my_l] = obuf[c, my_x, t]
            return
        for h in range(2):
            obuf[c, :, t, :, spans[h]] = product(spans[h])
            pass_on(c - 2, 1, t, h).start()

            @pl.when(inner)
            def _(h=h):
                rback[c - 2, t, my_l, :, spans[h]] = obuf[c, my_x, t, :, spans[h]]

            @pl.when(outer)
            def _(h=h):
                pass_on(c - 2, 0, t, h).start()

    def stage_u(r, t, h):
        @pl.when(inner)
        def _():
            for ld in near_l:
                remote(
                    obuf.at[2, 0, t, :, parts[h]], rback.at[r, t, ld, :, parts[h]],
                    bx_ss.at[0, 1, t, h], rb_rs.at[r, ld, t, h], at(*near[0]),
                ).wait_recv()
            rsum[r, t, :, spans[h]] = collect(1 + r, t, rback[r, t, :, :, spans[h]]).astype(BF)
            send_sum(r, t, h).start()

    def stage_g(q):
        span = slice(q * quarter, (q + 1) * quarter)
        all_g = recv[:, :, 1].reshape(n_exp * cap, cols)
        hq = hbuf[:, :, :, span].reshape(n_exp * cap, quarter)
        dg_o[span, :] = lax.dot_general(hq, all_g, TN, preferred_element_type=F32).astype(BF)

    def stage_p():
        for t in range(2):
            for ld in near_l:
                remote(
                    obuf.at[0, 0, t], bnear.at[t, ld], b_ss.at[0, 1, t], bn_rs.at[ld, t],
                    at(*near[0]),
                ).wait_recv()
            nsum[t] = collect(0, t, bnear[t])

    for load in loads[:4]:
        load.wait()
    meta[...] = jnp.concatenate(
        [ids_r[...].astype(F32), gate_r[...], jnp.zeros((8 - 2 * topk, n_tok), F32)], axis=0
    )
    prepare(0, ids_r[...].astype(F32), gate_r[...])
    near_step(0)
    @pl.when(inner)
    def _():
        pl.semaphore_wait(barrier, len(friends) + 1)

    @pl.when(outer)
    def _():
        pl.semaphore_wait(barrier, len(friends))

    send_meta().start()

    def stage_n(t):
        if t:
            near_step(t)
        for j in (2, 1, 0):
            send_near(j, t).start()

    def stage_t(t, role):
        @pl.when(role)
        def _():
            for h in range(2):
                send_block(t, h).start()

    stages = {
        "A": stage_a, "B": stage_b, "C": stage_c, "D": stage_d, "E": stage_e,
    }
    loaded = False
    for step in STEPS:
        if step[0] == "A" and not loaded:
            for load in loads[4:]:
                load.wait()
            loaded = True
        if step == "P":
            stage_p()
        elif step[0] == "N":
            stage_n("fb".index(step[1]))
        elif step[0] in "IO":
            stage_t("fb".index(step[1]), inner if step[0] == "I" else outer)
        elif step[0] == "G":
            stage_g(int(step[1]))
        else:
            t, c = "fb".index(step[1]), "NMAB".index(step[2])
            if step[0] == "S":
                stage_s(c - 2, t, int(step[3]))
            elif step[0] == "U":
                stage_u(c - 2, t, int(step[3]))
            else:
                stages[step[0]](c, t)

    outs = (mixed_o, tgrad_o)
    for t in range(2):
        for h in range(2):
            remote(
                rsum.at[0, t, :, parts[h]], fback.at[t, :, parts[h]], u_ss.at[0, t, h],
                fb_rs.at[t, h], at(far_z[0], my_x),
            ).wait_recv()
            outs[t][:, spans[h]] = (
                nsum[t, :, spans[h]] + fback[t, :, spans[h]].astype(F32)
            ).astype(BF)

    send_meta().wait_send()
    for t in range(2):
        for h in range(2):
            send_block(t, h).wait_send()
            for r in range(2):
                pass_on(r, 1, t, h).wait_send()
        for j in range(3):
            send_near(j, t).wait_send()
        for c in range(CHUNKS):
            for copy in (rs1(c, t), rs2(c, t), ag_y(c, t), ag_m(c, t), ag_r(c, t)):
                copy.wait_send()
        for c, j in ((0, 1), (1, 0), (1, 1)):
            give(c, j, t).wait_send()

    pieces = [(r, t, h) for r in range(2) for t in range(2) for h in range(2)]

    @pl.when(inner)
    def _():
        for r, t, h in pieces:
            for j in range(3):
                send_relay(r, j, t, h).wait_send()
            send_sum(r, t, h).wait_send()

    @pl.when(outer)
    def _():
        for r, t, h in pieces:
            pass_on(r, 0, t, h).wait_send()


def finish_kernel(mixed_r, tgrad_r, dg_r, mixed_o, tgrad_o, dg_o, sem):
    part = dg_r.shape[0] // CHUNKS
    spans = [pl.ds(i * part, part) for i in range(CHUNKS)]
    pairs = [(mixed_r, mixed_o), (tgrad_r, tgrad_o)]
    pairs += [(dg_r.at[span], dg_o.at[span]) for span in spans]
    copies = [pltpu.make_async_copy(a, b, sem.at[i]) for i, (a, b) in enumerate(pairs)]
    for copy in copies:
        copy.start()
    for copy in copies:
        copy.wait()


def fused(tokens, expert_ids, gates, cotangent, w_gate, w_up, w_down):
    n_tok, topk = expert_ids.shape
    cols = tokens.shape[1]
    hid = w_gate.shape[2]
    n_exp, n_sec = lax.axis_size("expert"), lax.axis_size("section")
    cap = capacity_of(n_tok, topk, n_exp)
    quarter = hid // n_sec
    group = n_exp // 2
    vm = pl.BlockSpec(memory_space=pltpu.VMEM)
    hbm = pl.BlockSpec(memory_space=pl.ANY)
    dma = pltpu.SemaphoreType.DMA
    ids_r, gate_r = expert_ids.T, gates.T
    shapes = (
        jax.ShapeDtypeStruct((n_tok, cols), BF),
        jax.ShapeDtypeStruct((n_tok, cols), BF),
        jax.ShapeDtypeStruct((hid, cols), BF),
    )

    def per(j, *lead):
        return pltpu.VMEM((n_exp, *lead, j, cap, quarter), BF)

    results = pl.pallas_call(
        functools.partial(expert_kernel, n_exp, cap),
        out_shape=shapes,
        in_specs=[pl.BlockSpec(memory_space=pltpu.HBM)] * 7,
        out_specs=(vm, vm, vm),
        scratch_shapes=[
            pltpu.VMEM((topk, n_tok), jnp.int32),
            pltpu.VMEM((topk, n_tok), F32),
            pltpu.VMEM((n_tok, cols), BF),
            pltpu.VMEM((n_tok, cols), BF),
            pltpu.VMEM((cols, hid), BF),
            pltpu.VMEM((cols, hid), BF),
            pltpu.VMEM((hid, cols), BF),
            pltpu.VMEM((8, n_tok), F32),
            pltpu.VMEM((2, 8, n_tok), F32),
            pltpu.VMEM((3, group * cap, n_tok), BF),
            pltpu.VMEM((3, group * cap, n_tok), BF),
            pltpu.VMEM((3, group * cap, n_tok), BF),
            pltpu.VMEM((3, group * cap, 1), F32),
            pltpu.VMEM((2, group, cap, cols), BF),
            pltpu.VMEM((CHUNKS, 2, 2, cap, cols), BF),
            pltpu.VMEM((2, 2, n_tok, cols), BF),
            pltpu.VMEM((2, 2, group, cap, cols), BF),
            per(2, 2, 2), per(1, 2, 2), per(2, 2), per(1, 2), per(2), per(1), per(2), per(1),
            per(1, 2, 2), per(2, 2, 2),
            pltpu.VMEM((n_exp, cap, quarter), F32),
            pltpu.VMEM((n_exp, cap, quarter), F32),
            pltpu.VMEM((CHUNKS, 2, cap, hid), BF),
            pltpu.VMEM((CHUNKS, 2, 2, cap, cols), BF),
            pltpu.VMEM((2, group, cap, cols), BF),
            pltpu.VMEM((2, 2, group, cap, cols), BF),
            pltpu.VMEM((2, 2, n_tok, cols), BF),
            pltpu.VMEM((2, n_tok, cols), BF),
            pltpu.VMEM((2, n_tok, cols), F32),
            dma((7,)), dma, dma((2,)), dma((3, 2)), dma((2, 2, 2)), dma((2, 2)),
            dma((2, 2, 2)), dma((2, 3, 2, 2)), dma((2, 2, 2, 2)),
        ]
        + [dma((2 * CHUNKS,)) for _ in range(10)]
        + [
            dma((2, 2, 2)), dma((2, 2, 2, 2)), dma((group, 2)), dma((2, group, 2, 2)),
            dma((2, 2, 2)), dma((2, 2)),
        ],
        compiler_params=pltpu.CompilerParams(
            collective_id=0, has_side_effects=True, vmem_limit_bytes=40 * 1024 * 1024
        ),
    )(
        *[
            pltpu.with_memory_space_constraint(x, pltpu.HBM)
            for x in (ids_r, gate_r, tokens, cotangent, w_gate[0], w_up[0], w_down[0])
        ]
    )
    mixed, tgrad, dg = pl.pallas_call(
        finish_kernel,
        out_shape=shapes,
        in_specs=[hbm] * 3,
        out_specs=(hbm,) * 3,
        scratch_shapes=[dma((CHUNKS + 2,))],
        compiler_params=pltpu.CompilerParams(vmem_limit_bytes=8 * 1024 * 1024),
    )(*results)
    return mixed, tgrad, dg[None]


def capacity_of(tok_rows, top_count, expert_count):
    return min(tok_rows, max(2, 3 * tok_rows * top_count // (2 * expert_count)))


def layer(tokens, expert_ids, *rest):
    n_exp, n_sec = lax.axis_size("expert"), lax.axis_size("section")
    n_tok, topk = expert_ids.shape
    cap = capacity_of(n_tok, topk, n_exp)
    hid = rest[2].shape[2]
    tiles = (
        n_exp == 2 * CHUNKS and n_sec == 4 and cap % 16 == 0 and n_tok % 128 == 0
        and tokens.shape[1] % 128 == 0 and hid % (n_sec * 128) == 0
    )
    return (fused if tiles else local)(tokens, expert_ids, *rest)


def solution(mesh):
    placed = (
        P("expert", "section"),
        P("expert", None),
        P("expert", None),
        P("expert", "section"),
        P("expert", "section", None),
        P("expert", "section", None),
        P("expert", None, "section"),
    )
    return jax.shard_map(
        layer,
        mesh=mesh,
        in_specs=placed,
        out_specs=(P("expert", "section"), P("expert", "section"), P("expert", None, "section")),
        check_vma=False,
    )
```
